128 devices in a mesh: gx: 4 (over z), gy: 32 (over y, x, core).
Axes of the slice: x: 4, y: 4, z: 4, core: 2. Of those that a mesh axis runs over, the one named last changes fastest.
Arguments:
- blocks: float32 [768, 128, 4096], P(('gx', 'gy')), may hold values from -0.046875 to 0.046875
- features: float32 [2048, 128, 512], P(('gx', 'gy')), may hold values from -6 to 6
- col_ids: int32 [768, 32], P(('gx', 'gy')), may hold values from 0 to 15
- row_ids: int32 [768], P(('gx', 'gy')), may hold values from 0 to 127
- factor: float32 [512, 512], replicated, may hold values from -0.25 to 0.25
Outputs:
- owned_rows: float32 [16384, 512], P(('gx', 'gy'))
- returned: float32 [98304, 512], P(('gx', 'gy'))
The draws below stay inside these ranges and needn't reach their ends.
Inputs may be any that keep to these rules, and one draw needn't show every extreme that they name: `row_ids`: row block r is owned by device r, counted over gx+gy with gx slowest. Row blocks are named with a power-law skew; one device may name a row block more than once. `col_ids`: indices into the device's own feature tiles.
All inputs are finite; a program needn't handle non-finite values.
Results may differ from the reference program's by a relative error of at most 0.00013.
Values sent between devices are 32-bit elements; how exact they have to be, the bound alone decides.
A program may use at most 192 MiB of HBM per device.

```python
import math
import jax
import jax.numpy as jnp
import numpy as np
from jax import lax

B = 128
FEAT = 512
SLOTS = 6
BPR = 32
FT = 16
ROWBLOCKS = 128
DEVICES = 128


def with_ends(array, own_key, smallest, largest):
    index_at = [jax.random.randint(jax.random.fold_in(own_key, axis), (), 0, length) for axis, length in enumerate(array.shape)]
    main_axis = array.shape.index(max(array.shape))
    beside = index_at[:main_axis] + [(index_at[main_axis] + 1) % array.shape[main_axis]] + index_at[main_axis + 1:]
    return array.at[tuple(index_at)].set(smallest).at[tuple(beside)].set(largest)


def block_scale(stream_key, shape, pieces, low, top_value):
    loudness, own = 1.0, jax.random.fold_in(stream_key, 6)
    for axis_at, shards_of in pieces:
        draws = jnp.exp(jax.random.uniform(jax.random.fold_in(own, axis_at), (shards_of,), jnp.float32, low / len(pieces), top_value / len(pieces)))
        loudness = loudness * jnp.repeat(draws, shape[axis_at] // shards_of).reshape([-1 if axis == axis_at else 1 for axis in range(len(shape))])
    return loudness


def rank_table(number_of, slope):
    portions = [(1 << 20) // math.isqrt(grade ** slope) + 1 for grade in range(1, number_of + 1)]
    spread = 1 + sum(portions) // (1 << 30)
    return np.cumsum(np.array([max(1, weight // spread) for weight in portions]))


def skewed_ids(own_key, extent, amount, slope):
    table = rank_table(amount, slope)
    ticket = jax.random.randint(jax.random.fold_in(own_key, 1), extent, 0, int(table[amount - 1]))
    standing = jnp.searchsorted(jnp.asarray(table, jnp.int32), ticket, side="right")
    return jax.random.permutation(jax.random.fold_in(own_key, 2), amount)[standing].astype(jnp.int32)


def gaussian(rng, extent, spread, reach, shards=(), kind=jnp.bfloat16):
    drawn = jax.random.normal(rng, extent, jnp.float32) * spread
    if len(shards) > 0:
        drawn = block_scale(rng, extent, shards, -0.22, 0.18) * drawn
    return jnp.clip(drawn, min=-reach, max=reach).astype(kind)


def setup_inputs(seed: int = 0) -> dict:
    key_list = jax.random.split(jax.random.key(seed), 6)
    blocks = gaussian(key_list[0], (DEVICES * SLOTS, B, BPR * B), (4 * BPR * B) ** -0.5, 0.046875, ((0, 128),), jnp.float32)
    features = gaussian(key_list[1], (DEVICES * FT, B, FEAT), 1.0, 6.0, ((0, 128),), jnp.float32)
    col_ids = with_ends(jax.random.randint(key_list[2], (DEVICES * SLOTS, BPR), 0, FT), jax.random.fold_in(key_list[2], 1), 0, FT - 1).astype(jnp.int32)
    row_ids = with_ends(skewed_ids(key_list[3], (DEVICES * SLOTS,), ROWBLOCKS, 2), jax.random.fold_in(key_list[3], 3), 0, ROWBLOCKS - 1).astype(jnp.int32)
    factor = gaussian(key_list[4], (FEAT, FEAT), FEAT ** -0.5, 0.25, (), jnp.float32)
    return dict(blocks=blocks, features=features, col_ids=col_ids, row_ids=row_ids, factor=factor)


HIGHEST = lax.Precision.HIGHEST


def reference(blocks, features, col_ids, row_ids, factor):
    dev_count = blocks.shape[0] // SLOTS
    blk_all = blocks.reshape(dev_count, SLOTS, B, BPR * B)
    feat_all = features.reshape(dev_count, FT, B, FEAT)
    col_all = col_ids.reshape(dev_count, SLOTS, BPR)

    def device_rows(packed):
        blk_rows, feat_rows, col_rows = packed
        gathered = feat_rows[col_rows].reshape(SLOTS, BPR * B, FEAT)
        return jnp.einsum("sik,skf->sif", blk_rows, gathered, precision=HIGHEST)

    partial_value = lax.map(device_rows, (blk_all, feat_all, col_all)).reshape(dev_count * SLOTS, B, FEAT)
    row_sums = jax.ops.segment_sum(partial_value, row_ids, num_segments=ROWBLOCKS)
    owned_rows = jnp.dot(jnp.tanh(row_sums).reshape(ROWBLOCKS * B, FEAT), factor,
                         precision=HIGHEST, preferred_element_type=jnp.float32)
    returned = owned_rows.reshape(ROWBLOCKS, B, FEAT)[row_ids].reshape(dev_count * SLOTS * B, FEAT)
    return owned_rows, returned
```

```python
import functools

import jax
import jax.numpy as jnp
from jax import lax
from jax.experimental import pallas as pl
from jax.experimental.pallas import tpu as pltpu
from jax.sharding import PartitionSpec as P

MESH = pl.DeviceIdType.MESH
F32 = jnp.float32
BF16 = jnp.bfloat16
I32 = jnp.int32

B = 128
FEAT = 512
SLOTS = 6
BPR = 32
FT = 16
HALF = B // 2
LANES = 128
GROUPS = FEAT // LANES
TILE_ROWS = HALF * GROUPS
SHIFT = {"z": 5, "y": 3, "x": 1}
PIECES = ((88, 0, "zyx"), (88, 88, "yxz"), (80, 176, "xzy"))


def split(value):
    high = value.astype(BF16)
    return high, (value - high.astype(F32)).astype(BF16)


def product(left_high, left_low, right_high, right_low):
    dot = functools.partial(jnp.dot, preferred_element_type=F32)
    return dot(left_high, right_high) + (dot(left_high, right_low) + dot(left_low, right_high))


def product_kernel(col_ids, row_ids, blocks, features, part, labels, total, f_high, f_low, a_high, a_low):
    k = pl.program_id(0)

    @pl.when(k == 0)
    def _():
        for t in range(FT):
            high, low = split(features[t])
            f_high[pl.ds(t * B, B), :] = high
            f_low[pl.ds(t * B, B), :] = low
        row = lax.broadcasted_iota(I32, (8, LANES), 0)
        tile = jnp.full((8, LANES), -1, I32)
        for s in range(SLOTS):
            tile = jnp.where(row == s, row_ids[s], tile)
        labels[...] = tile

    total[...] = jnp.zeros_like(total)
    for j in range(BPR):
        t = col_ids[k, j]
        total[t] += blocks[0, :, pl.ds(j * B, B)]
    for t in range(FT):
        high, low = split(total[t])
        a_high[:, pl.ds(t * B, B)] = high
        a_low[:, pl.ds(t * B, B)] = low
    result = product(a_high[...], a_low[...], f_high[...], f_low[...])
    for half in range(2):
        for g in range(GROUPS):
            part[half, 0, pl.ds(g * HALF, HALF), :] = result[
                half * HALF : (half + 1) * HALF, g * LANES : (g + 1) * LANES
            ]


def local_product(blocks, features, col_ids, row_ids):
    return pl.pallas_call(
        product_kernel,
        grid_spec=pltpu.PrefetchScalarGridSpec(
            num_scalar_prefetch=2,
            grid=(SLOTS,),
            in_specs=[
                pl.BlockSpec((1, B, BPR * B), lambda k, *_: (k, 0, 0)),
                pl.BlockSpec((FT, B, FEAT), lambda k, *_: (0, 0, 0), pipeline_mode=pl.Buffered(1)),
            ],
            out_specs=[
                pl.BlockSpec((2, 1, TILE_ROWS, LANES), lambda k, *_: (0, k, 0, 0)),
                pl.BlockSpec((8, LANES), lambda k, *_: (0, 0)),
            ],
            scratch_shapes=[
                pltpu.VMEM((FT, B, B), F32),
                pltpu.VMEM((FT * B, FEAT), BF16),
                pltpu.VMEM((FT * B, FEAT), BF16),
                pltpu.VMEM((B, FT * B), BF16),
                pltpu.VMEM((B, FT * B), BF16),
            ],
        ),
        out_shape=[
            jax.ShapeDtypeStruct((2, SLOTS, TILE_ROWS, LANES), F32),
            jax.ShapeDtypeStruct((8, LANES), I32),
        ],
        compiler_params=pltpu.CompilerParams(vmem_limit_bytes=48 << 20),
    )(col_ids, row_ids, blocks, features)


PIECE_BUFFERS = (
    ("entries", 64),
    ("sums", 65),
    ("a2_far_up", 4),
    ("a2_far_down", 4),
    ("a2_got_far_up", 4),
    ("a2_got_far_down", 4),
    ("a2_up", 8),
    ("a2_down", 8),
    ("a2_got_up", 8),
    ("a2_got_down", 8),
    ("quarter", 8),
    ("a3_got_far_up", 1),
    ("a3_got_far_down", 1),
    ("a3_up", 1),
    ("a3_down", 1),
    ("a3_got_up", 2),
    ("a3_got_down", 2),
    ("dense", 33),
    ("b1_far_up", 6),
    ("b1_far_down", 6),
    ("b1_got_far_up", 6),
    ("b1_got_far_down", 6),
    ("b1_up", 12),
    ("b1_down", 12),
    ("b1_got_up", 12),
    ("b1_got_down", 12),
    ("answers", 12),
)
N_PIECES = len(PIECES)
N_SEMS = 64 * N_PIECES
N_LOCAL = 16 * N_PIECES


class Piece:
    pass


def exchange_kernel(part, labels, factor, owned, returned, *scratch):
    scratch = list(scratch)
    pieces = []
    for number, (rows, start, order) in enumerate(PIECES):
        piece = Piece()
        piece.number, piece.rows, piece.start, piece.order = number, rows, start, order
        for name, _ in PIECE_BUFFERS:
            setattr(piece, name, scratch.pop(0))
        pieces.append(piece)
    lab, tab_v, tab, x_buf, y_buf, fac, fac_high, fac_low, send_sem, recv_sem, local_sem = scratch

    z = lax.axis_index("gx")
    gy = lax.axis_index("gy")
    core = gy % 2
    at = {"z": z, "y": gy // 8, "x": (gy // 2) % 4}

    def neighbour(axis, step):
        to = dict(at)
        to[axis] = (at[axis] + step) % 4
        return (to["z"], to["y"] * 8 + to["x"] * 2 + core)

    sibling = (z, gy - core + (1 - core))
    counts = {"remote": 0, "local": 0}
    sent = []

    def remote(source, target, device):
        n = counts["remote"]
        counts["remote"] += 1
        copy = pltpu.make_async_remote_copy(
            src_ref=source,
            dst_ref=target,
            send_sem=send_sem.at[n],
            recv_sem=recv_sem.at[n],
            device_id=device,
            device_id_type=MESH,
        )
        copy.start()
        sent.append(copy)
        return copy

    def local(source, target):
        n = counts["local"]
        counts["local"] += 1
        copy = pltpu.make_async_copy(source, target, local_sem.at[n])
        copy.start()
        return copy

    barrier = pltpu.get_barrier_semaphore()
    greeted = [sibling] + [neighbour(axis, step) for axis in "zyx" for step in (1, 3)]
    for device in greeted:
        pl.semaphore_signal(barrier, inc=1, device_id=device, device_id_type=MESH)
    own_labels = local(labels, lab.at[0, pl.ds(0, 8)])
    get_factor = local(factor, fac)
    for p in pieces:
        p.own = local(part.at[core, :, pl.ds(p.start, p.rows), :], p.entries.at[pl.ds(0, SLOTS)])
        p.sums[0] = jnp.zeros((p.rows, LANES), F32)
        p.dense[0] = jnp.zeros((p.rows, LANES), F32)
    pl.semaphore_wait(barrier, len(greeted))

    sibling_labels = remote(labels, lab.at[0, pl.ds(8, 8)], sibling)
    for p in pieces:
        p.other = remote(
            part.at[1 - core, :, pl.ds(p.start, p.rows), :], p.entries.at[pl.ds(8, SLOTS)], sibling
        )
    for p in pieces:
        p.up, p.down = neighbour(p.order[0], 1), neighbour(p.order[0], 3)
        p.list_up, p.list_down = {}, {}
        for turn in range(2):
            t_up, t_down = turn, 1 - turn
            p.list_up[0, t_up] = remote(
                part.at[core, pl.ds(3 * t_up, 3), pl.ds(p.start, p.rows), :],
                p.entries.at[pl.ds(16 + 3 * t_up, 3)],
                p.up,
            )
            p.list_down[0, t_down] = remote(
                part.at[core, pl.ds(3 * t_down, 3), pl.ds(p.start, p.rows), :],
                p.entries.at[pl.ds(32 + 3 * t_down, 3)],
                p.down,
            )
    own_labels.wait()
    sibling_labels.wait_recv()
    for p in pieces:
        j = p.number
        p.lab_up = remote(lab.at[0], lab.at[1 + 3 * j], p.up)
        p.lab_down = remote(lab.at[0], lab.at[2 + 3 * j], p.down)
    for p in pieces:
        p.other.wait_recv()
        for turn in range(2):
            t_up, t_down = turn, 1 - turn
            p.list_up[1, t_up] = remote(
                p.entries.at[pl.ds(8 + 3 * t_up, 3)], p.entries.at[pl.ds(24 + 3 * t_up, 3)], p.up
            )
            p.list_down[1, t_down] = remote(
                p.entries.at[pl.ds(8 + 3 * t_down, 3)], p.entries.at[pl.ds(40 + 3 * t_down, 3)], p.down
            )
    for p in pieces:
        p.lab_up.wait_recv()
        p.lab_far = remote(lab.at[1 + 3 * p.number], lab.at[3 + 3 * p.number], p.up)
    get_factor.wait()
    high, low = split(fac[...])
    fac_high[...] = high
    fac_low[...] = low
    for p in pieces:
        p.lab_down.wait_recv()
        p.lab_far.wait_recv()
        j = p.number
        first, second, third = p.order
        seen = jnp.concatenate([lab[0], lab[1 + 3 * j], lab[2 + 3 * j], lab[3 + 3 * j]], axis=0)
        row = lax.broadcasted_iota(I32, (64, LANES), 0)
        lane = lax.broadcasted_iota(I32, (64, LANES), 1)
        wanted = jnp.sum(jnp.where(row == lane, seen, 0), axis=0, keepdims=True)
        previous = jnp.max(
            jnp.where(jnp.logical_and(seen == wanted, row < lane), row + 1, 0), axis=0, keepdims=True
        )

        def step_of(order):
            return jnp.where(order == 1, 3, jnp.where(order == 2, 1, jnp.where(order == 3, 2, 0)))

        def order_of(step):
            return jnp.where(step == 0, 0, jnp.where(step == 3, 1, step + 1))

        named = (
            (at[first] << SHIFT[first])
            + (((at[second] + step_of((lane >> 3) & 3)) & 3) << SHIFT[second])
            + (((at[third] + step_of((lane >> 1) & 3)) & 3) << SHIFT[third])
            + (lane & 1)
        )
        last = jnp.max(jnp.where(seen == named, row + 1, 0), axis=0, keepdims=True)
        place = (
            1
            + order_of((((wanted >> SHIFT[second]) & 3) - at[second]) & 3) * 8
            + order_of((((wanted >> SHIFT[third]) & 3) - at[third]) & 3) * 2
            + (wanted & 1)
        )
        place = jnp.where(((wanted >> SHIFT[first]) & 3) == at[first], place, 0)
        line = lax.broadcasted_iota(I32, (8, LANES), 0)
        tab_v[j] = jnp.where(line == 0, previous, jnp.where(line == 1, last, place))
    for p in pieces:
        p.far_up, p.far_down = {}, {}
        for h in range(2):
            p.list_up[h, 0].wait_recv()
            p.far_up[h] = remote(
                p.entries.at[pl.ds(16 + 8 * h, 3)], p.entries.at[pl.ds(48 + 8 * h, 3)], p.up
            )
            p.list_down[h, 1].wait_recv()
            p.far_down[h] = remote(
                p.entries.at[pl.ds(35 + 8 * h, 3)], p.entries.at[pl.ds(51 + 8 * h, 3)], p.down
            )
    get_tab = local(tab_v, tab)
    get_tab.wait()

    def add_lists(p, order):
        def body(h, carry):
            for s in range(SLOTS):
                i = order * 16 + h * 8 + s
                p.sums[i + 1] = p.entries[i] + p.sums[tab[p.number, 0, i]]
            return carry

        lax.fori_loop(0, 2, body, 0)

    for p in pieces:
        p.own.wait()
        add_lists(p, 0)
    for p in pieces:
        p.list_up[0, 1].wait_recv()
        p.list_up[1, 1].wait_recv()
        add_lists(p, 1)
        p.list_down[0, 0].wait_recv()
        p.list_down[1, 0].wait_recv()
        add_lists(p, 2)

    def pick(p, r):
        return p.sums[tab[p.number, 1, r]]

    for p in pieces:
        for h in range(2):
            p.far_up[h].wait_recv()
            p.far_down[h].wait_recv()
        add_lists(p, 3)
        p.up, p.down = neighbour(p.order[1], 1), neighbour(p.order[1], 3)

        def far_body(m, carry, p=p):
            p.a2_far_up[m] = pick(p, 24 + m)
            p.a2_far_down[m] = pick(p, 28 + m)
            return carry

        lax.fori_loop(0, 4, far_body, 0)

        def near_body(m, carry, p=p):
            p.a2_up[m + 4] = pick(p, 20 + m)
            p.a2_down[m] = pick(p, 8 + m)
            return carry

        lax.fori_loop(0, 4, near_body, 0)
        p.a2_far = (
            remote(p.a2_far_up, p.a2_got_far_up, p.up),
            remote(p.a2_far_down, p.a2_got_far_down, p.down),
        )
        p.a2_near = [
            remote(p.a2_up.at[pl.ds(4, 4)], p.a2_got_up.at[pl.ds(4, 4)], p.up),
            remote(p.a2_down.at[pl.ds(0, 4)], p.a2_got_down.at[pl.ds(0, 4)], p.down),
        ]
    for p in pieces:
        p.a2_far[0].wait_recv()

        def up_body(m, carry, p=p):
            p.a2_up[m] = p.a2_got_far_up[m] + pick(p, 16 + m)
            return carry

        lax.fori_loop(0, 4, up_body, 0)
        p.a2_near.append(remote(p.a2_up.at[pl.ds(0, 4)], p.a2_got_up.at[pl.ds(0, 4)], p.up))
        p.a2_far[1].wait_recv()

        def down_body(m, carry, p=p):
            p.a2_down[m + 4] = p.a2_got_far_down[m] + pick(p, 12 + m)
            return carry

        lax.fori_loop(0, 4, down_body, 0)
        p.a2_near.append(remote(p.a2_down.at[pl.ds(4, 4)], p.a2_got_down.at[pl.ds(4, 4)], p.down))

    for p in pieces:
        for copy in p.a2_near:
            copy.wait_recv()

        def quarter_body(m, carry, p=p):
            p.quarter[m] = pick(p, m) + (p.a2_got_up[m] + p.a2_got_down[m])
            return carry

        lax.fori_loop(0, 8, quarter_body, 0)
        p.up, p.down = neighbour(p.order[2], 1), neighbour(p.order[2], 3)
        p.a3_far = (
            remote(p.quarter.at[6], p.a3_got_far_up.at[0], p.up),
            remote(p.quarter.at[7], p.a3_got_far_down.at[0], p.down),
        )
        p.a3_near = [
            remote(p.quarter.at[5], p.a3_got_up.at[1], p.up),
            remote(p.quarter.at[2], p.a3_got_down.at[0], p.down),
        ]
    for p in pieces:
        p.a3_far[0].wait_recv()
        p.a3_up[0] = p.quarter[4] + p.a3_got_far_up[0]
        p.a3_far[1].wait_recv()
        p.a3_down[0] = p.quarter[3] + p.a3_got_far_down[0]
        p.a3_near.append(remote(p.a3_up.at[0], p.a3_got_up.at[0], p.up))
        p.a3_near.append(remote(p.a3_down.at[0], p.a3_got_down.at[1], p.down))
    for p in pieces:
        for copy in p.a3_near:
            copy.wait_recv()
        for b in range(2):
            x_buf[b, pl.ds(p.start, p.rows), :] = jnp.tanh(
                p.quarter[b] + (p.a3_got_up[b] + p.a3_got_down[b])
            )

    x = jnp.concatenate(
        [
            jnp.concatenate([x_buf[b, pl.ds(g * HALF, HALF), :] for g in range(GROUPS)], axis=1)
            for b in range(2)
        ],
        axis=0,
    )
    x_high, x_low = split(x)
    y = product(x_high, x_low, fac_high[...], fac_low[...])
    for b in range(2):
        rows_y = y[b * HALF : (b + 1) * HALF]
        y_buf[b] = rows_y
        flat = jnp.concatenate([rows_y[:, g * LANES : (g + 1) * LANES] for g in range(GROUPS)], axis=0)
        for p in pieces:
            p.dense[1 + b] = flat[p.start : p.start + p.rows]

    for p in pieces:
        d = p.dense
        p.b3 = {}
        p.b3["up", 0] = remote(d.at[1], d.at[3], p.up)
        p.b3["down", 1] = remote(d.at[2], d.at[6], p.down)
        p.b3["up", 1] = remote(d.at[2], d.at[4], p.up)
        p.b3["down", 0] = remote(d.at[1], d.at[5], p.down)
    half_rows = pl.ds(pl.multiple_of(core * HALF, HALF), HALF)
    keep = local(y_buf.at[core], owned.at[half_rows, :])
    give = remote(y_buf.at[1 - core], owned.at[half_rows, :], sibling)
    for p in pieces:
        d = p.dense
        p.b3["up", 0].wait_recv()
        p.b3["far", 0] = remote(d.at[3], d.at[7], p.up)
        p.b3["down", 1].wait_recv()
        p.b3["far", 1] = remote(d.at[6], d.at[8], p.down)
    for p in pieces:
        d = p.dense
        for key in (("up", 1), ("down", 0), ("far", 0), ("far", 1)):
            p.b3[key].wait_recv()
        p.up, p.down = neighbour(p.order[1], 1), neighbour(p.order[1], 3)
        p.b2 = {}
        p.b2["up", 0] = remote(d.at[pl.ds(1, 4)], d.at[pl.ds(9, 4)], p.up)
        p.b2["down", 1] = remote(d.at[pl.ds(5, 4)], d.at[pl.ds(21, 4)], p.down)
        p.b2["up", 1] = remote(d.at[pl.ds(5, 4)], d.at[pl.ds(13, 4)], p.up)
        p.b2["down", 0] = remote(d.at[pl.ds(1, 4)], d.at[pl.ds(17, 4)], p.down)
    for p in pieces:
        d = p.dense
        p.b2["up", 0].wait_recv()
        p.b2["far", 0] = remote(d.at[pl.ds(9, 4)], d.at[pl.ds(25, 4)], p.up)
        p.b2["down", 1].wait_recv()
        p.b2["far", 1] = remote(d.at[pl.ds(21, 4)], d.at[pl.ds(29, 4)], p.down)

    def answer(p, i):
        return p.dense[tab[p.number, 2, i]]

    for p in pieces:
        for key in (("up", 1), ("down", 0), ("far", 0), ("far", 1)):
            p.b2[key].wait_recv()
        p.up, p.down = neighbour(p.order[0], 1), neighbour(p.order[0], 3)

        def far_body(h, carry, p=p):
            for s in range(3):
                p.b1_far_up[h * 3 + s] = answer(p, 48 + h * 8 + s)
                p.b1_far_down[h * 3 + s] = answer(p, 51 + h * 8 + s)
            return carry

        lax.fori_loop(0, 2, far_body, 0)
        p.b1_far = (
            remote(p.b1_far_up, p.b1_got_far_up, p.up),
            remote(p.b1_far_down, p.b1_got_far_down, p.down),
        )

        def near_body(h, carry, p=p):
            for s in range(3):
                p.b1_up[6 + h * 3 + s] = answer(p, 35 + h * 8 + s)
                p.b1_down[h * 3 + s] = answer(p, 16 + h * 8 + s)
            return carry

        lax.fori_loop(0, 2, near_body, 0)
        p.b1_near = [
            remote(p.b1_up.at[pl.ds(6, 6)], p.b1_got_up.at[pl.ds(6, 6)], p.up),
            remote(p.b1_down.at[pl.ds(0, 6)], p.b1_got_down.at[pl.ds(0, 6)], p.down),
        ]
    for p in pieces:
        p.b1_far[0].wait_recv()

        def up_body(h, carry, p=p):
            for s in range(3):
                p.b1_up[h * 3 + s] = p.b1_got_far_up[h * 3 + s] + answer(p, 32 + h * 8 + s)
            return carry

        lax.fori_loop(0, 2, up_body, 0)
        p.b1_near.append(remote(p.b1_up.at[pl.ds(0, 6)], p.b1_got_up.at[pl.ds(0, 6)], p.up))
        p.b1_far[1].wait_recv()

        def down_body(h, carry, p=p):
            for s in range(3):
                p.b1_down[6 + h * 3 + s] = p.b1_got_far_down[h * 3 + s] + answer(p, 19 + h * 8 + s)
            return carry

        lax.fori_loop(0, 2, down_body, 0)
        p.b1_near.append(remote(p.b1_down.at[pl.ds(6, 6)], p.b1_got_down.at[pl.ds(6, 6)], p.down))
    last_local, last_remote = [], []
    for p in pieces:
        for copy in p.b1_near:
            copy.wait_recv()

        def answer_body(h, carry, p=p):
            for t in range(2):
                for s in range(3):
                    q = t * 6 + h * 3 + s
                    p.answers[h * 6 + t * 3 + s] = answer(p, h * 8 + t * 3 + s) + (
                        p.b1_got_up[q] + p.b1_got_down[q]
                    )
            return carry

        lax.fori_loop(0, 2, answer_body, 0)
        first_row = p.start
        while first_row < p.start + p.rows:
            g, r = divmod(first_row, HALF)
            n = min(HALF - r, p.start + p.rows - first_row)
            target = returned.at[
                :, pl.ds(pl.multiple_of(core * HALF + r, 8), n), pl.ds(g * LANES, LANES)
            ]
            here = pl.ds(first_row - p.start, n)
            last_remote.append(remote(p.answers.at[pl.ds(6, 6), here, :], target, sibling))
            last_local.append(local(p.answers.at[pl.ds(0, 6), here, :], target))
            first_row += n
    keep.wait()
    give.wait_recv()
    for copy in last_local:
        copy.wait()
    for copy in last_remote:
        copy.wait_recv()
    for copy in sent:
        copy.wait_send()


def exchange(part, labels, factor):
    scratch = []
    for rows, _, _ in PIECES:
        for _, depth in PIECE_BUFFERS:
            scratch.append(pltpu.VMEM((depth, rows, LANES), F32))
    scratch += [
        pltpu.VMEM((1 + 3 * N_PIECES, 16, LANES), I32),
        pltpu.VMEM((N_PIECES, 8, LANES), I32),
        pltpu.SMEM((N_PIECES, 8, LANES), I32),
        pltpu.VMEM((2, TILE_ROWS, LANES), F32),
        pltpu.VMEM((2, HALF, FEAT), F32),
        pltpu.VMEM((FEAT, FEAT), F32),
        pltpu.VMEM((FEAT, FEAT), BF16),
        pltpu.VMEM((FEAT, FEAT), BF16),
        pltpu.SemaphoreType.DMA((N_SEMS,)),
        pltpu.SemaphoreType.DMA((N_SEMS,)),
        pltpu.SemaphoreType.DMA((N_LOCAL,)),
    ]
    hbm = pl.BlockSpec(memory_space=pl.ANY)
    return pl.pallas_call(
        exchange_kernel,
        in_specs=[hbm] * 3,
        out_specs=[hbm] * 2,
        out_shape=[
            jax.ShapeDtypeStruct((B, FEAT), F32),
            jax.ShapeDtypeStruct((SLOTS, B, FEAT), F32),
        ],
        scratch_shapes=scratch,
        compiler_params=pltpu.CompilerParams(
            collective_id=0, has_side_effects=True, vmem_limit_bytes=60 << 20
        ),
    )(part, labels, factor)


def local_step(blocks, features, col_ids, row_ids, factor):
    part, labels = local_product(blocks, features, col_ids, row_ids)
    owned, returned = exchange(part, labels, factor)
    return owned, returned.reshape(SLOTS * B, FEAT)


def solution(mesh):
    return jax.shard_map(
        local_step,
        mesh=mesh,
        in_specs=(
            P(("gx", "gy"), None, None),
            P(("gx", "gy"), None, None),
            P(("gx", "gy"), None),
            P(("gx", "gy")),
            P(),
        ),
        out_specs=(P(("gx", "gy"), None), P(("gx", "gy"), None)),
        check_vma=False,
    )
```

```python
import functools

import jax
import jax.numpy as jnp
from jax import lax
from jax.experimental import pallas as pl
from jax.experimental.pallas import tpu as pltpu
from jax.sharding import PartitionSpec as P

MESH = pl.DeviceIdType.MESH
F32 = jnp.float32
BF16 = jnp.bfloat16
I32 = jnp.int32

B = 128
FEAT = 512
SLOTS = 6
BPR = 32
FT = 16
HALF = B // 2
STREAMS = 2
ROWS = HALF // STREAMS
LANES = 128
GROUPS = FEAT // LANES
TILE_ROWS = ROWS * GROUPS
SHIFT = {"z": 5, "y": 3, "x": 1}
ORDERS = ("zyx", "yxz", "xzy")
PIECES = (((0, 48), (48, 40), (88, 40)), ((0, 40), (40, 48), (88, 40)))
PAIRS = SLOTS // 2
FAR_UP = ((0, 0), (1, 0), (0, 1))
FAR_DOWN = ((1, 1), (0, 2), (1, 2))


def split(value):
    high = value.astype(BF16)
    return high, (value - high.astype(F32)).astype(BF16)


def product(left_high, left_low, right_high, right_low):
    dot = functools.partial(jnp.dot, preferred_element_type=F32)
    return dot(left_high, right_high) + (dot(left_high, right_low) + dot(left_low, right_high))


PIECE_BUFFERS = (
    ("sums", 49),
    ("a2_far_up", 4),
    ("a2_far_down", 4),
    ("a2_got_far_up", 4),
    ("a2_got_far_down", 4),
    ("a2_up", 8),
    ("a2_down", 8),
    ("a2_got_up", 8),
    ("a2_got_down", 8),
    ("quarter", 8),
    ("a3_got_far_up", 1),
    ("a3_got_far_down", 1),
    ("a3_up", 1),
    ("a3_down", 1),
    ("a3_got_up", 2),
    ("a3_got_down", 2),
    ("dense", 33),
    ("b1_far_up", 6),
    ("b1_far_down", 6),
    ("b1_got_far_up", 6),
    ("b1_got_far_down", 6),
    ("b1_up", 12),
    ("b1_down", 12),
    ("b1_got_up", 12),
    ("b1_got_down", 12),
)
N_REMOTE = 320
N_LOCAL = 32
RING = 4


class Piece:
    pass


def slot_place(pair, half):
    return half * SLOTS + 2 * pair


def kernel(blocks, features, col_ids, row_ids, factor, owned, returned, *scratch):
    scratch = list(scratch)
    streams = []
    for u in range(STREAMS):
        pieces = []
        for number, (start, rows) in enumerate(PIECES[u]):
            piece = Piece()
            piece.number, piece.start, piece.rows, piece.order = number, start, rows, ORDERS[number]
            piece.stream = u
            for name, _ in PIECE_BUFFERS:
                setattr(piece, name, scratch.pop(0))
            pieces.append(piece)
        streams.append(pieces)
    (
        blk, feat, f_high, f_low, chain, a_high, a_low, part, entries, cols, col_v, col_tab, ids,
        tile, lab, tab_v, tab, x_buf, y_buf, out_buf, fac, fac_high, fac_low,
        send_sem, recv_sem, local_sem,
    ) = scratch

    z = lax.axis_index("gx")
    gy = lax.axis_index("gy")
    core = gy % 2
    at = {"z": z, "y": gy // 8, "x": (gy // 2) % 4}

    def neighbour(axis, step):
        to = dict(at)
        to[axis] = (at[axis] + step) % 4
        return (to["z"], to["y"] * 8 + to["x"] * 2 + core)

    sibling = (z, gy - core + (1 - core))
    counts = {"remote": 0, "local": 0}
    sent = []

    def remote(source, target, device):
        n = counts["remote"]
        counts["remote"] += 1
        assert n < N_REMOTE
        copy = pltpu.make_async_remote_copy(
            src_ref=source,
            dst_ref=target,
            send_sem=send_sem.at[n],
            recv_sem=recv_sem.at[n],
            device_id=device,
            device_id_type=MESH,
        )
        copy.start()
        sent.append(copy)
        return copy

    def local(source, target):
        n = counts["local"]
        counts["local"] += 1
        assert n < N_LOCAL
        copy = pltpu.make_async_copy(source, target, local_sem.at[n])
        copy.start()
        return copy

    barrier = pltpu.get_barrier_semaphore()
    greeted = [sibling] + [neighbour(axis, step) for axis in "zyx" for step in (1, 3)]
    for device in greeted:
        pl.semaphore_signal(barrier, inc=1, device_id=device, device_id_type=MESH)
    get_cols = local(col_ids, cols)
    get_ids = local(row_ids, ids)
    get_feat = [local(features.at[pl.ds(4 * i, 4)], feat.at[pl.ds(4 * i, 4)]) for i in range(2)]
    get_blk = {k: local(blocks.at[k], blk.at[k % RING]) for k in range(2)}
    get_feat += [local(features.at[pl.ds(4 * i, 4)], feat.at[pl.ds(4 * i, 4)]) for i in range(2, 4)]
    for k in range(2, RING):
        get_blk[k] = local(blocks.at[k], blk.at[k % RING])
    get_factor = local(factor, fac)

    get_cols.wait()
    row = lax.broadcasted_iota(I32, (BPR, BPR), 0)
    lane = lax.broadcasted_iota(I32, (BPR, BPR), 1)
    for k in range(SLOTS):
        across = jnp.broadcast_to(cols[pl.ds(k, 1), :], (BPR, BPR))
        down = jnp.sum(jnp.where(row == lane, across, 0), axis=1, keepdims=True)
        col_v[pl.ds(2 * k, 1), pl.ds(0, BPR)] = jnp.max(
            jnp.where(jnp.logical_and(down == across, row < lane), row + 1, 0), axis=0, keepdims=True
        )
        col_v[pl.ds(2 * k + 1, 1), pl.ds(0, BPR)] = jnp.max(
            jnp.where(down == lane, row + 1, 0), axis=0, keepdims=True
        )
    get_ids.wait()
    line = lax.broadcasted_iota(I32, (8, LANES), 0)
    names = jnp.full((8, LANES), -1, I32)
    for s in range(SLOTS):
        names = jnp.where(line == s, ids[s], names)
    tile[...] = names
    chain[0] = jnp.zeros((B, B), F32)
    for pieces in streams:
        for p in pieces:
            p.sums[0] = jnp.zeros((p.rows, LANES), F32)
            p.dense[0] = jnp.zeros((p.rows, LANES), F32)

    def convert(first):
        def body(t, carry):
            high, low = split(feat[t])
            f_high[pl.ds(pl.multiple_of(t * B, B), B), :] = high
            f_low[pl.ds(pl.multiple_of(t * B, B), B), :] = low
            return carry

        lax.fori_loop(first, first + 4, body, 0)

    get_feat[0].wait()
    convert(0)
    get_col_tab = local(col_v, col_tab)
    get_feat[1].wait()
    convert(4)
    get_col_tab.wait()

    def gather_sums(k):
        get_blk[k].wait()
        held = blk.at[k % RING]

        for j in range(BPR):
            chain[j + 1] = held[:, pl.ds(j * B, B)] + chain[col_tab[2 * k, j]]
        for t in range(FT):
            high, low = split(chain[col_tab[2 * k + 1, t]])
            a_high[pl.ds((k % 2) * B, B), pl.ds(t * B, B)] = high
            a_low[pl.ds((k % 2) * B, B), pl.ds(t * B, B)] = low
        if k + RING < SLOTS:
            get_blk[k + RING] = local(blocks.at[k + RING], blk.at[k % RING])

    def multiply(pair):
        result = product(a_high[...], a_low[...], f_high[...], f_low[...])
        for s in range(2):
            for half in range(2):
                for u in range(STREAMS):
                    first = s * B + half * HALF + u * ROWS
                    for g in range(GROUPS):
                        part[2 * pair + s, half, u, pl.ds(g * ROWS, ROWS), :] = result[
                            first : first + ROWS, g * LANES : (g + 1) * LANES
                        ]

    give_part = {}

    def send_part(pair):
        give_part[pair] = remote(
            part.at[pl.ds(2 * pair, 2), 1 - core], entries.at[pl.ds(slot_place(pair, 1), 2)], sibling
        )

    def send_list(pieces, half, pair):
        for p in pieces:
            here = pl.ds(p.start, p.rows)
            if half == 0:
                source = part.at[pl.ds(2 * pair, 2), core, p.stream, here]
            else:
                source = entries.at[pl.ds(slot_place(pair, 1), 2), p.stream, here]
            for name, order, to in (("up", 1, 1), ("down", 2, 3)):
                target = entries.at[pl.ds(order * 12 + slot_place(pair, half), 2), p.stream, here]
                p.lists[name, half, pair] = remote(source, target, neighbour(p.order[0], to))

    def send_far(pieces, name, half, pair):
        order, to = (1, 1) if name == "up" else (2, 3)
        for p in pieces:
            here = pl.ds(p.start, p.rows)
            p.lists[name, half, pair].wait_recv()
            p.far[half, pair] = remote(
                entries.at[pl.ds(order * 12 + slot_place(pair, half), 2), p.stream, here],
                entries.at[pl.ds(36 + slot_place(pair, half), 2), p.stream, here],
                neighbour(p.order[0], to),
            )

    for pieces in streams:
        for p in pieces:
            p.lists, p.far = {}, {}
    first_stream, second_stream = streams

    gather_sums(0)
    pl.semaphore_wait(barrier, len(greeted))
    give_names = remote(tile, lab.at[0, pl.ds(8, 8)], sibling)
    keep_names = local(tile, lab.at[0, pl.ds(0, 8)])
    get_feat[2].wait()
    convert(8)
    get_feat[3].wait()
    convert(12)
    gather_sums(1)
    multiply(0)
    send_part(0)
    send_list(first_stream, 0, 0)
    send_list(second_stream, 0, 0)
    keep_names.wait()
    give_names.wait_recv()
    lab_up, lab_down, lab_far = {}, {}, {}
    for j in range(3):
        lab_up[j] = remote(lab.at[0], lab.at[1 + 3 * j], neighbour(ORDERS[j][0], 1))
        lab_down[j] = remote(lab.at[0], lab.at[2 + 3 * j], neighbour(ORDERS[j][0], 3))
    gather_sums(2)
    give_part[0].wait_recv()
    send_list(first_stream, 1, 0)
    send_list(second_stream, 1, 0)
    gather_sums(3)
    multiply(1)
    send_part(1)
    send_list(first_stream, 0, 1)
    send_list(second_stream, 0, 1)
    for j in range(3):
        lab_up[j].wait_recv()
        lab_far[j] = remote(lab.at[1 + 3 * j], lab.at[3 + 3 * j], neighbour(ORDERS[j][0], 1))
    gather_sums(4)
    give_part[1].wait_recv()
    send_list(first_stream, 1, 1)
    send_list(second_stream, 1, 1)
    gather_sums(5)
    multiply(2)
    send_part(2)
    send_list(first_stream, 0, 2)
    send_far(first_stream, "up", 0, 0)
    send_far(first_stream, "up", 1, 0)
    give_part[2].wait_recv()
    send_list(first_stream, 1, 2)
    send_list(second_stream, 0, 2)
    send_list(second_stream, 1, 2)

    def make_table(j):
        lab_down[j].wait_recv()
        lab_far[j].wait_recv()
        first, second, third = ORDERS[j]
        seen = jnp.concatenate([lab[0], lab[1 + 3 * j], lab[2 + 3 * j], lab[3 + 3 * j]], axis=0)
        row = lax.broadcasted_iota(I32, (64, LANES), 0)
        lane = lax.broadcasted_iota(I32, (64, LANES), 1)
        place_of_row = (row >> 4) * 12 + ((row >> 3) & 1) * 6 + (row & 7) + 1
        wanted = jnp.sum(jnp.where(row == lane, seen, 0), axis=0, keepdims=True)
        previous = jnp.max(
            jnp.where(jnp.logical_and(seen == wanted, row < lane), place_of_row, 0),
            axis=0,
            keepdims=True,
        )

        def step_of(order):
            return jnp.where(order == 1, 3, jnp.where(order == 2, 1, jnp.where(order == 3, 2, 0)))

        def order_of(step):
            return jnp.where(step == 0, 0, jnp.where(step == 3, 1, step + 1))

        named = (
            (at[first] << SHIFT[first])
            + (((at[second] + step_of((lane >> 3) & 3)) & 3) << SHIFT[second])
            + (((at[third] + step_of((lane >> 1) & 3)) & 3) << SHIFT[third])
            + (lane & 1)
        )
        last = jnp.max(jnp.where(seen == named, place_of_row, 0), axis=0, keepdims=True)
        place = (
            1
            + order_of((((wanted >> SHIFT[second]) & 3) - at[second]) & 3) * 8
            + order_of((((wanted >> SHIFT[third]) & 3) - at[third]) & 3) * 2
            + (wanted & 1)
        )
        place = jnp.where(((wanted >> SHIFT[first]) & 3) == at[first], place, 0)
        tab_v[j] = jnp.where(line == 0, previous, jnp.where(line == 1, last, place))

    for j in range(3):
        make_table(j)
    send_far(first_stream, "up", 0, 1)
    send_far(first_stream, "down", 1, 1)
    get_tab = local(tab_v, tab)
    send_far(first_stream, "down", 0, 2)
    send_far(second_stream, "up", 0, 0)
    send_far(second_stream, "up", 1, 0)
    send_far(first_stream, "down", 1, 2)
    get_tab.wait()

    def add_lists(pieces, order):
        for p in pieces:
            here = pl.ds(p.start, p.rows)
            for h in range(2):
                for s in range(SLOTS):
                    place = order * 12 + h * 6 + s
                    if order == 0 and h == 0:
                        value = part[s, core, p.stream, here]
                    else:
                        value = entries[place, p.stream, here]
                    p.sums[place + 1] = value + p.sums[tab[p.number, 0, order * 16 + h * 8 + s]]

    def add_near_lists(pieces):
        add_lists(pieces, 0)
        for p in pieces:
            for half in range(2):
                for pair in range(PAIRS):
                    if (half, pair) not in FAR_UP:
                        p.lists["up", half, pair].wait_recv()
                    if (half, pair) not in FAR_DOWN:
                        p.lists["down", half, pair].wait_recv()
        add_lists(pieces, 1)
        add_lists(pieces, 2)

    def pick(p, r):
        return p.sums[tab[p.number, 1, r]]

    def loop(n, body):
        def step(m, carry):
            body(m)
            return carry

        lax.fori_loop(0, n, step, 0)

    def a2_far(pieces):
        for p in pieces:
            for chunk in FAR_UP + FAR_DOWN:
                p.far[chunk].wait_recv()
            add_lists([p], 3)
            p.up, p.down = neighbour(p.order[1], 1), neighbour(p.order[1], 3)

            def body(m, p=p):
                p.a2_far_up[m] = pick(p, 24 + m)
                p.a2_far_down[m] = pick(p, 28 + m)

            loop(4, body)
            p.a2_far = (
                remote(p.a2_far_up, p.a2_got_far_up, p.up),
                remote(p.a2_far_down, p.a2_got_far_down, p.down),
            )

    def a2_near(pieces):
        for p in pieces:

            def body(m, p=p):
                p.a2_up[m + 4] = pick(p, 20 + m)
                p.a2_down[m] = pick(p, 8 + m)

            loop(4, body)
            p.a2_near = [
                remote(p.a2_up.at[pl.ds(4, 4)], p.a2_got_up.at[pl.ds(4, 4)], p.up),
                remote(p.a2_down.at[pl.ds(0, 4)], p.a2_got_down.at[pl.ds(0, 4)], p.down),
            ]

    def a2_merge(pieces):
        for p in pieces:
            p.a2_far[0].wait_recv()

            def up_body(m, p=p):
                p.a2_up[m] = p.a2_got_far_up[m] + pick(p, 16 + m)

            loop(4, up_body)
            p.a2_near.append(remote(p.a2_up.at[pl.ds(0, 4)], p.a2_got_up.at[pl.ds(0, 4)], p.up))
            p.a2_far[1].wait_recv()

            def down_body(m, p=p):
                p.a2_down[m + 4] = p.a2_got_far_down[m] + pick(p, 12 + m)

            loop(4, down_body)
            p.a2_near.append(
                remote(p.a2_down.at[pl.ds(4, 4)], p.a2_got_down.at[pl.ds(4, 4)], p.down)
            )

    def a3_start(pieces):
        for p in pieces:
            for copy in p.a2_near:
                copy.wait_recv()

            def body(m, p=p):
                p.quarter[m] = pick(p, m) + (p.a2_got_up[m] + p.a2_got_down[m])

            loop(8, body)
            p.up, p.down = neighbour(p.order[2], 1), neighbour(p.order[2], 3)
            p.a3_far = (
                remote(p.quarter.at[6], p.a3_got_far_up.at[0], p.up),
                remote(p.quarter.at[7], p.a3_got_far_down.at[0], p.down),
            )
            p.a3_near = [
                remote(p.quarter.at[5], p.a3_got_up.at[1], p.up),
                remote(p.quarter.at[2], p.a3_got_down.at[0], p.down),
            ]

    def a3_merge(pieces):
        for p in pieces:
            p.a3_far[0].wait_recv()
            p.a3_up[0] = p.quarter[4] + p.a3_got_far_up[0]
            p.a3_far[1].wait_recv()
            p.a3_down[0] = p.quarter[3] + p.a3_got_far_down[0]
            p.a3_near.append(remote(p.a3_up.at[0], p.a3_got_up.at[0], p.up))
            p.a3_near.append(remote(p.a3_down.at[0], p.a3_got_down.at[1], p.down))

    def a3_end(pieces):
        for p in pieces:
            for copy in p.a3_near:
                copy.wait_recv()
            for b in range(2):
                x_buf[p.stream, b, pl.ds(p.start, p.rows), :] = jnp.tanh(
                    p.quarter[b] + (p.a3_got_up[b] + p.a3_got_down[b])
                )

    give_owned, last_local = [], []

    def update(pieces):
        u = pieces[0].stream
        x = jnp.concatenate(
            [
                jnp.concatenate(
                    [x_buf[u, b, pl.ds(g * ROWS, ROWS), :] for g in range(GROUPS)], axis=1
                )
                for b in range(2)
            ],
            axis=0,
        )
        x_high, x_low = split(x)
        y = product(x_high, x_low, fac_high[...], fac_low[...])
        for b in range(2):
            rows_y = y[b * ROWS : (b + 1) * ROWS]
            y_buf[u, b] = rows_y
            flat = jnp.concatenate(
                [rows_y[:, g * LANES : (g + 1) * LANES] for g in range(GROUPS)], axis=0
            )
            for p in pieces:
                p.dense[1 + b] = flat[p.start : p.start + p.rows]
        for p in pieces:
            d = p.dense
            p.b3 = {}
            p.b3["up", 0] = remote(d.at[1], d.at[3], p.up)
            p.b3["down", 1] = remote(d.at[2], d.at[6], p.down)
            p.b3["up", 1] = remote(d.at[2], d.at[4], p.up)
            p.b3["down", 0] = remote(d.at[1], d.at[5], p.down)
        here = pl.ds(pl.multiple_of(core * HALF + u * ROWS, ROWS), ROWS)
        last_local.append(local(y_buf.at[u, core], owned.at[here, :]))
        give_owned.append(remote(y_buf.at[u, 1 - core], owned.at[here, :], sibling))

    def b3_far(pieces):
        for p in pieces:
            d = p.dense
            p.b3["up", 0].wait_recv()
            p.b3["far", 0] = remote(d.at[3], d.at[7], p.up)
            p.b3["down", 1].wait_recv()
            p.b3["far", 1] = remote(d.at[6], d.at[8], p.down)

    def b2_start(pieces):
        for p in pieces:
            d = p.dense
            for key in (("up", 1), ("down", 0), ("far", 0), ("far", 1)):
                p.b3[key].wait_recv()
            p.up, p.down = neighbour(p.order[1], 1), neighbour(p.order[1], 3)
            p.b2 = {}
            p.b2["up", 0] = remote(d.at[pl.ds(1, 4)], d.at[pl.ds(9, 4)], p.up)
            p.b2["down", 1] = remote(d.at[pl.ds(5, 4)], d.at[pl.ds(21, 4)], p.down)
            p.b2["up", 1] = remote(d.at[pl.ds(5, 4)], d.at[pl.ds(13, 4)], p.up)
            p.b2["down", 0] = remote(d.at[pl.ds(1, 4)], d.at[pl.ds(17, 4)], p.down)

    def b2_far(pieces):
        for p in pieces:
            d = p.dense
            p.b2["up", 0].wait_recv()
            p.b2["far", 0] = remote(d.at[pl.ds(9, 4)], d.at[pl.ds(25, 4)], p.up)
            p.b2["down", 1].wait_recv()
            p.b2["far", 1] = remote(d.at[pl.ds(21, 4)], d.at[pl.ds(29, 4)], p.down)

    def answer(p, i):
        return p.dense[tab[p.number, 2, i]]

    def b1_far(pieces):
        for p in pieces:
            for key in (("up", 1), ("down", 0), ("far", 0), ("far", 1)):
                p.b2[key].wait_recv()
            p.up, p.down = neighbour(p.order[0], 1), neighbour(p.order[0], 3)

            def body(h, p=p):
                for s in range(3):
                    p.b1_far_up[h * 3 + s] = answer(p, 48 + h * 8 + s)
                    p.b1_far_down[h * 3 + s] = answer(p, 51 + h * 8 + s)

            loop(2, body)
            p.b1_far = (
                remote(p.b1_far_up, p.b1_got_far_up, p.up),
                remote(p.b1_far_down, p.b1_got_far_down, p.down),
            )

    def b1_near(pieces):
        for p in pieces:

            def body(h, p=p):
                for s in range(3):
                    p.b1_up[6 + h * 3 + s] = answer(p, 35 + h * 8 + s)
                    p.b1_down[h * 3 + s] = answer(p, 16 + h * 8 + s)

            loop(2, body)
            p.b1_near = [
                remote(p.b1_up.at[pl.ds(6, 6)], p.b1_got_up.at[pl.ds(6, 6)], p.up),
                remote(p.b1_down.at[pl.ds(0, 6)], p.b1_got_down.at[pl.ds(0, 6)], p.down),
            ]

    def b1_merge(pieces):
        for p in pieces:
            p.b1_far[0].wait_recv()

            def up_body(h, p=p):
                for s in range(3):
                    p.b1_up[h * 3 + s] = p.b1_got_far_up[h * 3 + s] + answer(p, 32 + h * 8 + s)

            loop(2, up_body)
            p.b1_near.append(remote(p.b1_up.at[pl.ds(0, 6)], p.b1_got_up.at[pl.ds(0, 6)], p.up))
            p.b1_far[1].wait_recv()

            def down_body(h, p=p):
                for s in range(3):
                    p.b1_down[6 + h * 3 + s] = p.b1_got_far_down[h * 3 + s] + answer(p, 19 + h * 8 + s)

            loop(2, down_body)
            p.b1_near.append(
                remote(p.b1_down.at[pl.ds(6, 6)], p.b1_got_down.at[pl.ds(6, 6)], p.down)
            )

    last_remote = []

    def finish(pieces):
        u = pieces[0].stream
        for p in pieces:
            for copy in p.b1_near:
                copy.wait_recv()

            def body(h, p=p):
                for t in range(2):
                    for s in range(3):
                        q = t * 6 + h * 3 + s
                        value = answer(p, h * 8 + t * 3 + s) + (p.b1_got_up[q] + p.b1_got_down[q])
                        done = 0
                        while done < p.rows:
                            g, r = divmod(p.start + done, ROWS)
                            n = min(ROWS - r, p.rows - done)
                            out_buf[u, h * 6 + t * 3 + s, pl.ds(r, n), pl.ds(g * LANES, LANES)] = value[
                                done : done + n
                            ]
                            done += n

            loop(2, body)
        here = pl.ds(pl.multiple_of(core * HALF + u * ROWS, ROWS), ROWS)
        last_remote.append(
            remote(out_buf.at[u, pl.ds(6, 6)], returned.at[:, here, :], sibling)
        )
        last_local.append(local(out_buf.at[u, pl.ds(0, 6)], returned.at[:, here, :]))

    get_factor.wait()
    high, low = split(fac[...])
    fac_high[...] = high
    fac_low[...] = low
    add_near_lists(first_stream)
    a2_far(first_stream)
    a2_near(first_stream)
    for name, chunks in (("up", FAR_UP[2:]), ("down", FAR_DOWN)):
        for chunk in chunks:
            send_far(second_stream, name, *chunk)
    add_near_lists(second_stream)
    a2_far(second_stream)
    a2_merge(first_stream)
    a2_near(second_stream)
    a2_merge(second_stream)
    a3_start(first_stream)
    a3_merge(first_stream)
    a3_start(second_stream)
    a3_end(first_stream)
    a3_merge(second_stream)
    update(first_stream)
    a3_end(second_stream)
    update(second_stream)
    b3_far(first_stream)
    b2_start(first_stream)
    b3_far(second_stream)
    b2_far(first_stream)
    b2_start(second_stream)
    b2_far(second_stream)
    b1_far(first_stream)
    b1_near(first_stream)
    b1_far(second_stream)
    b1_merge(first_stream)
    b1_near(second_stream)
    b1_merge(second_stream)
    finish(first_stream)
    finish(second_stream)
    for copy in last_local:
        copy.wait()
    for copy in give_owned + last_remote:
        copy.wait_recv()
    for copy in sent:
        copy.wait_send()


def local_step(blocks, features, col_ids, row_ids, factor):
    scratch = []
    for u in range(STREAMS):
        for _, rows in PIECES[u]:
            for _, depth in PIECE_BUFFERS:
                scratch.append(pltpu.VMEM((depth, rows, LANES), F32))
    scratch += [
        pltpu.VMEM((RING, B, BPR * B), F32),
        pltpu.VMEM((FT, B, FEAT), F32),
        pltpu.VMEM((FT * B, FEAT), BF16),
        pltpu.VMEM((FT * B, FEAT), BF16),
        pltpu.VMEM((BPR + 1, B, B), F32),
        pltpu.VMEM((2 * B, FT * B), BF16),
        pltpu.VMEM((2 * B, FT * B), BF16),
        pltpu.VMEM((SLOTS, 2, STREAMS, TILE_ROWS, LANES), F32),
        pltpu.VMEM((48, STREAMS, TILE_ROWS, LANES), F32),
        pltpu.VMEM((SLOTS, BPR), I32),
        pltpu.VMEM((16, LANES), I32),
        pltpu.SMEM((16, LANES), I32),
        pltpu.SMEM((SLOTS,), I32),
        pltpu.VMEM((8, LANES), I32),
        pltpu.VMEM((10, 16, LANES), I32),
        pltpu.VMEM((3, 8, LANES), I32),
        pltpu.SMEM((3, 8, LANES), I32),
        pltpu.VMEM((STREAMS, 2, TILE_ROWS, LANES), F32),
        pltpu.VMEM((STREAMS, 2, ROWS, FEAT), F32),
        pltpu.VMEM((STREAMS, 2 * SLOTS, ROWS, FEAT), F32),
        pltpu.VMEM((FEAT, FEAT), F32),
        pltpu.VMEM((FEAT, FEAT), BF16),
        pltpu.VMEM((FEAT, FEAT), BF16),
        pltpu.SemaphoreType.DMA((N_REMOTE,)),
        pltpu.SemaphoreType.DMA((N_REMOTE,)),
        pltpu.SemaphoreType.DMA((N_LOCAL,)),
    ]
    hbm = pl.BlockSpec(memory_space=pl.ANY)
    owned, returned = pl.pallas_call(
        kernel,
        in_specs=[hbm] * 5,
        out_specs=[hbm] * 2,
        out_shape=[
            jax.ShapeDtypeStruct((B, FEAT), F32),
            jax.ShapeDtypeStruct((SLOTS, B, FEAT), F32),
        ],
        scratch_shapes=scratch,
        compiler_params=pltpu.CompilerParams(
            collective_id=0, has_side_effects=True, vmem_limit_bytes=67043328
        ),
    )(blocks, features, col_ids, row_ids, factor)
    return owned, returned.reshape(SLOTS * B, FEAT)


def solution(mesh):
    return jax.shard_map(
        local_step,
        mesh=mesh,
        in_specs=(
            P(("gx", "gy"), None, None),
            P(("gx", "gy"), None, None),
            P(("gx", "gy"), None),
            P(("gx", "gy")),
            P(),
        ),
        out_specs=(P(("gx", "gy"), None), P(("gx", "gy"), None)),
        check_vma=False,
    )
```

```python
import functools

import jax
import jax.numpy as jnp
from jax import lax
from jax.experimental import pallas as pl
from jax.experimental.pallas import tpu as pltpu
from jax.sharding import PartitionSpec as P

MESH = pl.DeviceIdType.MESH
F32 = jnp.float32
BF16 = jnp.bfloat16
I32 = jnp.int32

B = 128
FEAT = 512
SLOTS = 6
BPR = 32
FT = 16
HALF = B // 2
STREAMS = 2
ROWS = HALF // STREAMS
LANES = 128
GROUPS = FEAT // LANES
TILE_ROWS = ROWS * GROUPS
SHIFT = {"z": 5, "y": 3, "x": 1}
ORDERS = ("zyx", "yxz", "xzy")
PIECES = (((0, 48), (48, 40), (88, 40)), ((0, 40), (40, 48), (88, 40)))
CHUNKS = ((0, 1), (1, 1), (2, 2), (4, 2))
FAR_UP = ((0, 0), (1, 0), (0, 1), (1, 1), (0, 3))
FAR_DOWN = ((0, 2), (1, 2), (1, 3))


def split(value):
    high = value.astype(BF16)
    return high, (value - high.astype(F32)).astype(BF16)


def product(left_high, left_low, right_high, right_low):
    dot = functools.partial(jnp.dot, preferred_element_type=F32)
    return dot(left_high, right_high) + (dot(left_high, right_low) + dot(left_low, right_high))


PIECE_BUFFERS = (
    ("sums", 49),
    ("a2_far_up", 4),
    ("a2_far_down", 4),
    ("a2_got_far_up", 4),
    ("a2_got_far_down", 4),
    ("a2_up", 8),
    ("a2_down", 8),
    ("a2_got", 16),
    ("quarter", 8),
    ("a3_got_far", 2),
    ("a3_up", 1),
    ("a3_down", 1),
    ("a3_got", 4),
    ("dense", 33),
    ("b1_got_far_up", 6),
    ("b1_got_far_down", 6),
    ("b1_got", 24),
)
PIECE_SLOTS = 36 + 24 + 6 + 6 + 24 + 36
N_SEND = 32
N_RECV = 176
N_LOCAL = 20
RING = 4
VMEM_LIMIT = 62 << 20


class Piece:
    pass


def kernel(blocks, features, col_ids, row_ids, factor, out, *scratch):
    scratch = list(scratch)
    streams = []
    for u in range(STREAMS):
        pieces = []
        for number, (start, rows) in enumerate(PIECES[u]):
            piece = Piece()
            piece.number, piece.start, piece.rows, piece.order = number, start, rows, ORDERS[number]
            piece.stream = u
            for name, _ in PIECE_BUFFERS:
                setattr(piece, name, scratch.pop(0))
            piece.b1_far_up, piece.b1_far_down = piece.sums.at[pl.ds(1, 6)], piece.sums.at[pl.ds(7, 6)]
            piece.b1_up, piece.b1_down = piece.sums.at[pl.ds(13, 12)], piece.sums.at[pl.ds(25, 12)]
            piece.slots_sent = 0
            pieces.append(piece)
        streams.append(pieces)
    (
        blk, feat, f_high, f_low, chain, a_high, a_low, part, entries, cols, col_v, col_tab, ids,
        tile, lab, tab_v, tab, x_buf, y_buf, out_buf, fac, fac_high, fac_low,
        send_sem, recv_sem, local_sem,
    ) = scratch

    z = lax.axis_index("gx")
    gy = lax.axis_index("gy")
    core = gy % 2
    at = {"z": z, "y": gy // 8, "x": (gy // 2) % 4}

    def neighbour(axis, step):
        to = dict(at)
        to[axis] = (at[axis] + step) % 4
        return (to["z"], to["y"] * 8 + to["x"] * 2 + core)

    sibling = (z, gy - core + (1 - core))
    counts = {"send": 0, "recv": 0, "local": 0}
    sent = []

    def take(kind, limit):
        n = counts[kind]
        counts[kind] += 1
        assert n < limit
        return n

    def arrival():
        return recv_sem.at[take("recv", N_RECV)]

    for pieces in streams:
        for p in pieces:
            p.send = send_sem.at[take("send", N_SEND)]

    def remote(source, target, device, piece=None, recv=None):
        copy = pltpu.make_async_remote_copy(
            src_ref=source,
            dst_ref=target,
            send_sem=send_sem.at[take("send", N_SEND)] if piece is None else piece.send,
            recv_sem=arrival() if recv is None else recv,
            device_id=device,
            device_id_type=MESH,
        )
        copy.start()
        if piece is None:
            sent.append(copy)
        else:
            piece.slots_sent += source.shape[0] if len(source.shape) == 3 else 1
        return copy

    def wait_all(ref, sem):
        pltpu.make_async_copy(ref, ref, sem).wait()

    def local(source, target):
        copy = pltpu.make_async_copy(source, target, local_sem.at[take("local", N_LOCAL)])
        copy.start()
        return copy

    barrier = pltpu.get_barrier_semaphore()
    greeted = [sibling] + [neighbour(axis, step) for axis in "zyx" for step in (1, 3)]
    for device in greeted:
        pl.semaphore_signal(barrier, inc=1, device_id=device, device_id_type=MESH)
    get_cols = local(col_ids, cols)
    get_ids = local(row_ids, ids)
    get_feat = [local(features.at[pl.ds(0, 8)], feat.at[pl.ds(0, 8)])]
    get_blk = {0: local(blocks.at[0], blk.at[0])}
    get_feat.append(local(features.at[pl.ds(8, 8)], feat.at[pl.ds(8, 8)]))
    for k in range(1, RING):
        get_blk[k] = local(blocks.at[k], blk.at[k])
    get_factor = local(factor, fac)

    get_cols.wait()
    row = lax.broadcasted_iota(I32, (BPR, BPR), 0)
    lane = lax.broadcasted_iota(I32, (BPR, BPR), 1)
    for k in range(SLOTS):
        across = jnp.broadcast_to(cols[pl.ds(k, 1), :], (BPR, BPR))
        down = jnp.sum(jnp.where(row == lane, across, 0), axis=1, keepdims=True)
        col_v[pl.ds(2 * k, 1), pl.ds(0, BPR)] = jnp.max(
            jnp.where(jnp.logical_and(down == across, row < lane), row + 1, 0), axis=0, keepdims=True
        )
        col_v[pl.ds(2 * k + 1, 1), pl.ds(0, BPR)] = jnp.max(
            jnp.where(down == lane, row + 1, 0), axis=0, keepdims=True
        )
    get_ids.wait()
    line = lax.broadcasted_iota(I32, (8, LANES), 0)
    names = jnp.full((8, LANES), -1, I32)
    for s in range(SLOTS):
        names = jnp.where(line == s, ids[s], names)
    tile[...] = names
    chain[0] = jnp.zeros((B, B), F32)
    for pieces in streams:
        for p in pieces:
            p.sums[0] = jnp.zeros((p.rows, LANES), F32)
            p.dense[0] = jnp.zeros((p.rows, LANES), F32)

    get_col_tab = local(col_v, col_tab)

    def convert(first):
        def body(t, carry):
            high, low = split(feat[t])
            f_high[pl.ds(pl.multiple_of(t * B, B), B), :] = high
            f_low[pl.ds(pl.multiple_of(t * B, B), B), :] = low
            return carry

        lax.fori_loop(first, first + 8, body, 0)

    def gather_sums(k):
        get_blk[k].wait()
        held = blk.at[k % RING]

        for j in range(BPR):
            chain[j + 1] = held[:, pl.ds(j * B, B)] + chain[col_tab[2 * k, j]]
        for t in range(FT):
            high, low = split(chain[col_tab[2 * k + 1, t]])
            a_high[:, pl.ds(t * B, B)] = high
            a_low[:, pl.ds(t * B, B)] = low
        if k + RING < SLOTS:
            get_blk[k + RING] = local(blocks.at[k + RING], blk.at[k % RING])

    def make(k):
        gather_sums(k)
        result = product(a_high[...], a_low[...], f_high[...], f_low[...])
        for half in range(2):
            for u in range(STREAMS):
                first = half * HALF + u * ROWS
                for g in range(GROUPS):
                    part[k, half, u, pl.ds(g * ROWS, ROWS), :] = result[
                        first : first + ROWS, g * LANES : (g + 1) * LANES
                    ]

    give_part = {}

    def place_of(half, chunk):
        return half * SLOTS + CHUNKS[chunk][0]

    def send_part(chunk):
        first, number = CHUNKS[chunk]
        give_part[chunk] = remote(
            part.at[pl.ds(first, number), 1 - core],
            entries.at[pl.ds(place_of(1, chunk), number)],
            sibling,
        )

    WAYS = {"up": (1, 1), "down": (2, 3)}

    def send_list(pieces, half, chunk):
        first, number = CHUNKS[chunk]
        for p in pieces:
            here = pl.ds(p.start, p.rows)
            if half == 0:
                source = part.at[pl.ds(first, number), core, p.stream, here]
            else:
                source = entries.at[pl.ds(place_of(1, chunk), number), p.stream, here]
            for name, far in (("up", FAR_UP), ("down", FAR_DOWN)):
                order, to = WAYS[name]
                target = entries.at[pl.ds(order * 12 + place_of(half, chunk), number), p.stream, here]
                recv = None if (half, chunk) in far else p.list_recv
                p.lists[name, half, chunk] = remote(source, target, neighbour(p.order[0], to), p, recv)

    def send_far(pieces, half, chunk):
        name = "up" if (half, chunk) in FAR_UP else "down"
        order, to = WAYS[name]
        number = CHUNKS[chunk][1]
        for p in pieces:
            here = pl.ds(p.start, p.rows)
            p.lists[name, half, chunk].wait_recv()
            remote(
                entries.at[pl.ds(order * 12 + place_of(half, chunk), number), p.stream, here],
                entries.at[pl.ds(36 + place_of(half, chunk), number), p.stream, here],
                neighbour(p.order[0], to),
                p,
                p.far_recv,
            )

    for pieces in streams:
        for p in pieces:
            p.lists = {}
            p.list_recv, p.far_recv = arrival(), arrival()
    one, two = streams

    get_feat[0].wait()
    convert(0)
    get_feat[1].wait()
    convert(8)
    get_col_tab.wait()
    make(0)
    pl.semaphore_wait(barrier, len(greeted))
    give_names = remote(tile, lab.at[0, pl.ds(8, 8)], sibling)
    keep_names = local(tile, lab.at[0, pl.ds(0, 8)])
    send_part(0)
    send_list(one, 0, 0)
    send_list(two, 0, 0)
    make(1)
    send_part(1)
    give_part[0].wait_recv()
    send_list(one, 1, 0)
    send_list(two, 1, 0)
    send_list(one, 0, 1)
    send_list(two, 0, 1)
    keep_names.wait()
    give_names.wait_recv()
    lab_up, lab_down, lab_far = {}, {}, {}
    for j in range(3):
        lab_up[j] = remote(lab.at[0], lab.at[1 + 3 * j], neighbour(ORDERS[j][0], 1))
        lab_down[j] = remote(lab.at[0], lab.at[2 + 3 * j], neighbour(ORDERS[j][0], 3))
    make(2)
    give_part[1].wait_recv()
    send_list(one, 1, 1)
    send_list(two, 1, 1)
    make(3)
    send_part(2)
    send_list(one, 0, 2)
    send_far(one, 0, 0)
    send_far(one, 1, 0)
    make(4)
    give_part[2].wait_recv()
    send_list(one, 1, 2)
    for j in range(3):
        lab_up[j].wait_recv()
        lab_far[j] = remote(lab.at[1 + 3 * j], lab.at[3 + 3 * j], neighbour(ORDERS[j][0], 1))
    make(5)
    send_part(3)
    send_list(one, 0, 3)
    send_far(one, 0, 1)
    send_far(one, 1, 1)
    send_far(one, 0, 2)
    give_part[3].wait_recv()
    send_list(one, 1, 3)
    send_far(one, 1, 2)
    send_list(two, 0, 2)
    send_list(two, 1, 2)
    for chunk in FAR_UP[:4]:
        send_far(two, *chunk)

    def make_table(j):
        lab_down[j].wait_recv()
        lab_far[j].wait_recv()
        first, second, third = ORDERS[j]
        seen = jnp.concatenate([lab[0], lab[1 + 3 * j], lab[2 + 3 * j], lab[3 + 3 * j]], axis=0)
        row = lax.broadcasted_iota(I32, (64, LANES), 0)
        lane = lax.broadcasted_iota(I32, (64, LANES), 1)
        place_of_row = (row >> 4) * 12 + ((row >> 3) & 1) * 6 + (row & 7) + 1
        wanted = jnp.sum(jnp.where(row == lane, seen, 0), axis=0, keepdims=True)
        previous = jnp.max(
            jnp.where(jnp.logical_and(seen == wanted, row < lane), place_of_row, 0),
            axis=0,
            keepdims=True,
        )

        def step_of(order):
            return jnp.where(order == 1, 3, jnp.where(order == 2, 1, jnp.where(order == 3, 2, 0)))

        def order_of(step):
            return jnp.where(step == 0, 0, jnp.where(step == 3, 1, step + 1))

        named = (
            (at[first] << SHIFT[first])
            + (((at[second] + step_of((lane >> 3) & 3)) & 3) << SHIFT[second])
            + (((at[third] + step_of((lane >> 1) & 3)) & 3) << SHIFT[third])
            + (lane & 1)
        )
        last = jnp.max(jnp.where(seen == named, place_of_row, 0), axis=0, keepdims=True)
        place = (
            1
            + order_of((((wanted >> SHIFT[second]) & 3) - at[second]) & 3) * 8
            + order_of((((wanted >> SHIFT[third]) & 3) - at[third]) & 3) * 2
            + (wanted & 1)
        )
        place = jnp.where(((wanted >> SHIFT[first]) & 3) == at[first], place, 0)
        tab_v[j] = jnp.where(line == 0, previous, jnp.where(line == 1, last, place))

    for j in range(3):
        make_table(j)
    send_far(one, 0, 3)
    send_far(one, 1, 3)
    get_tab = local(tab_v, tab)
    send_list(two, 0, 3)
    send_list(two, 1, 3)
    get_tab.wait()

    def add_lists(pieces, order):
        for p in pieces:
            here = pl.ds(p.start, p.rows)
            for h in range(2):
                for s in range(SLOTS):
                    place = order * 12 + h * 6 + s
                    if order == 0 and h == 0:
                        value = part[s, core, p.stream, here]
                    else:
                        value = entries[place, p.stream, here]
                    p.sums[place + 1] = value + p.sums[tab[p.number, 0, order * 16 + h * 8 + s]]

    def add_near_lists(pieces):
        add_lists(pieces, 0)
        for p in pieces:
            wait_all(p.sums.at[pl.ds(0, 12)], p.list_recv)
        add_lists(pieces, 1)
        add_lists(pieces, 2)

    def pick(p, r):
        return p.sums[tab[p.number, 1, r]]

    def loop(n, body):
        def step(m, carry):
            body(m)
            return carry

        lax.fori_loop(0, n, step, 0)

    def a2_far(pieces):
        for p in pieces:
            wait_all(p.sums.at[pl.ds(0, 12)], p.far_recv)
            add_lists([p], 3)
            p.up, p.down = neighbour(p.order[1], 1), neighbour(p.order[1], 3)

            def body(m, p=p):
                p.a2_far_up[m] = pick(p, 24 + m)
                p.a2_far_down[m] = pick(p, 28 + m)

            loop(4, body)
            p.a2_far = (
                remote(p.a2_far_up, p.a2_got_far_up, p.up, p),
                remote(p.a2_far_down, p.a2_got_far_down, p.down, p),
            )
            p.a2_recv = arrival()

    def a2_near(pieces):
        for p in pieces:

            def body(m, p=p):
                p.a2_up[m + 4] = pick(p, 20 + m)
                p.a2_down[m] = pick(p, 8 + m)

            loop(4, body)
            remote(p.a2_up.at[pl.ds(4, 4)], p.a2_got.at[pl.ds(4, 4)], p.up, p, p.a2_recv)
            remote(p.a2_down.at[pl.ds(0, 4)], p.a2_got.at[pl.ds(8, 4)], p.down, p, p.a2_recv)

    def a2_merge(pieces):
        for p in pieces:
            p.a2_far[0].wait_recv()

            def up_body(m, p=p):
                p.a2_up[m] = p.a2_got_far_up[m] + pick(p, 16 + m)

            loop(4, up_body)
            remote(p.a2_up.at[pl.ds(0, 4)], p.a2_got.at[pl.ds(0, 4)], p.up, p, p.a2_recv)
            p.a2_far[1].wait_recv()

            def down_body(m, p=p):
                p.a2_down[m + 4] = p.a2_got_far_down[m] + pick(p, 12 + m)

            loop(4, down_body)
            remote(p.a2_down.at[pl.ds(4, 4)], p.a2_got.at[pl.ds(12, 4)], p.down, p, p.a2_recv)

    def a3_start(pieces):
        for p in pieces:
            wait_all(p.a2_got, p.a2_recv)

            def body(m, p=p):
                p.quarter[m] = pick(p, m) + (p.a2_got[m] + p.a2_got[8 + m])

            loop(8, body)
            p.up, p.down = neighbour(p.order[2], 1), neighbour(p.order[2], 3)
            p.a3_far = (
                remote(p.quarter.at[6], p.a3_got_far.at[0], p.up, p),
                remote(p.quarter.at[7], p.a3_got_far.at[1], p.down, p),
            )
            p.a3_recv = arrival()
            remote(p.quarter.at[5], p.a3_got.at[1], p.up, p, p.a3_recv)
            remote(p.quarter.at[2], p.a3_got.at[2], p.down, p, p.a3_recv)

    def a3_merge(pieces):
        for p in pieces:
            p.a3_far[0].wait_recv()
            p.a3_up[0] = p.quarter[4] + p.a3_got_far[0]
            p.a3_far[1].wait_recv()
            p.a3_down[0] = p.quarter[3] + p.a3_got_far[1]
            remote(p.a3_up.at[0], p.a3_got.at[0], p.up, p, p.a3_recv)
            remote(p.a3_down.at[0], p.a3_got.at[3], p.down, p, p.a3_recv)

    def a3_end(pieces):
        for p in pieces:
            wait_all(p.a3_got, p.a3_recv)
            for b in range(2):
                x_buf[p.stream, b, pl.ds(p.start, p.rows), :] = jnp.tanh(
                    p.quarter[b] + (p.a3_got[b] + p.a3_got[2 + b])
                )

    last = []

    def update(pieces):
        u = pieces[0].stream
        x = jnp.concatenate(
            [
                jnp.concatenate(
                    [x_buf[u, b, pl.ds(g * ROWS, ROWS), :] for g in range(GROUPS)], axis=1
                )
                for b in range(2)
            ],
            axis=0,
        )
        x_high, x_low = split(x)
        y = product(x_high, x_low, fac_high[...], fac_low[...])
        for b in range(2):
            rows_y = y[b * ROWS : (b + 1) * ROWS]
            flat = jnp.concatenate(
                [rows_y[:, g * LANES : (g + 1) * LANES] for g in range(GROUPS)], axis=0
            )
            for p in pieces:
                p.dense[1 + b] = flat[p.start : p.start + p.rows]
        for p in pieces:
            d = p.dense
            p.b3_recv = arrival()
            p.b3_up = remote(d.at[1], d.at[3], p.up, p)
            p.b3_down = remote(d.at[2], d.at[6], p.down, p)
            remote(d.at[2], d.at[4], p.up, p, p.b3_recv)
            remote(d.at[1], d.at[5], p.down, p, p.b3_recv)
        here = pl.ds(pl.multiple_of(core * HALF + u * ROWS, ROWS), ROWS)
        mine = jnp.where(core == 0, y[:ROWS], y[ROWS:])
        y_buf[u] = jnp.where(core == 0, y[ROWS:], y[:ROWS])
        out[0, here, :] = mine
        last.append(remote(y_buf.at[u], out.at[0, here, :], sibling))

    def b3_far(pieces):
        for p in pieces:
            d = p.dense
            p.b3_up.wait_recv()
            remote(d.at[3], d.at[7], p.up, p, p.b3_recv)
            p.b3_down.wait_recv()
            remote(d.at[6], d.at[8], p.down, p, p.b3_recv)

    def b2_start(pieces):
        for p in pieces:
            d = p.dense
            wait_all(d.at[pl.ds(5, 4)], p.b3_recv)
            p.up, p.down = neighbour(p.order[1], 1), neighbour(p.order[1], 3)
            p.b2_recv = arrival()
            p.b2_up = remote(d.at[pl.ds(1, 4)], d.at[pl.ds(9, 4)], p.up, p)
            p.b2_down = remote(d.at[pl.ds(5, 4)], d.at[pl.ds(21, 4)], p.down, p)
            remote(d.at[pl.ds(5, 4)], d.at[pl.ds(13, 4)], p.up, p, p.b2_recv)
            remote(d.at[pl.ds(1, 4)], d.at[pl.ds(17, 4)], p.down, p, p.b2_recv)

    def b2_far(pieces):
        for p in pieces:
            d = p.dense
            p.b2_up.wait_recv()
            remote(d.at[pl.ds(9, 4)], d.at[pl.ds(25, 4)], p.up, p, p.b2_recv)
            p.b2_down.wait_recv()
            remote(d.at[pl.ds(21, 4)], d.at[pl.ds(29, 4)], p.down, p, p.b2_recv)

    def answer(p, i):
        return p.dense[tab[p.number, 2, i]]

    def b1_far(pieces):
        for p in pieces:
            wait_all(p.dense.at[pl.ds(17, 16)], p.b2_recv)
            p.up, p.down = neighbour(p.order[0], 1), neighbour(p.order[0], 3)

            def body(h, p=p):
                for s in range(3):
                    p.b1_far_up[h * 3 + s] = answer(p, 48 + h * 8 + s)
                    p.b1_far_down[h * 3 + s] = answer(p, 51 + h * 8 + s)

            loop(2, body)
            p.b1_far = (
                remote(p.b1_far_up, p.b1_got_far_up, p.up, p),
                remote(p.b1_far_down, p.b1_got_far_down, p.down, p),
            )
            p.b1_recv = arrival()

    def b1_near(pieces):
        for p in pieces:

            def body(h, p=p):
                for s in range(3):
                    p.b1_up[6 + h * 3 + s] = answer(p, 35 + h * 8 + s)
                    p.b1_down[h * 3 + s] = answer(p, 16 + h * 8 + s)

            loop(2, body)
            remote(p.b1_up.at[pl.ds(6, 6)], p.b1_got.at[pl.ds(6, 6)], p.up, p, p.b1_recv)
            remote(p.b1_down.at[pl.ds(0, 6)], p.b1_got.at[pl.ds(12, 6)], p.down, p, p.b1_recv)

    def b1_merge(pieces):
        for p in pieces:
            p.b1_far[0].wait_recv()

            def up_body(h, p=p):
                for s in range(3):
                    p.b1_up[h * 3 + s] = p.b1_got_far_up[h * 3 + s] + answer(p, 32 + h * 8 + s)

            loop(2, up_body)
            remote(p.b1_up.at[pl.ds(0, 6)], p.b1_got.at[pl.ds(0, 6)], p.up, p, p.b1_recv)
            p.b1_far[1].wait_recv()

            def down_body(h, p=p):
                for s in range(3):
                    p.b1_down[6 + h * 3 + s] = p.b1_got_far_down[h * 3 + s] + answer(p, 19 + h * 8 + s)

            loop(2, down_body)
            remote(p.b1_down.at[pl.ds(6, 6)], p.b1_got.at[pl.ds(18, 6)], p.down, p, p.b1_recv)

    def finish(pieces):
        u = pieces[0].stream
        first = core * HALF + u * ROWS
        for p in pieces:
            wait_all(p.b1_got, p.b1_recv)

            def body(n, p=p):
                t, s = n // 3, n % 3
                for h in (1, 0):
                    q = t * 6 + h * 3 + s
                    value = answer(p, h * 8 + n) + (p.b1_got[q] + p.b1_got[12 + q])
                    done = 0
                    while done < p.rows:
                        g, r = divmod(p.start + done, ROWS)
                        size = min(ROWS - r, p.rows - done)
                        across = pl.ds(g * LANES, LANES)
                        if h == 0:
                            rows = pl.ds(pl.multiple_of(first + r, 8), size)
                            out[1 + n, rows, across] = value[done : done + size]
                        else:
                            out_buf[u, n, pl.ds(r, size), across] = value[done : done + size]
                        done += size

            loop(SLOTS, body)
        here = pl.ds(pl.multiple_of(first, ROWS), ROWS)
        last.append(remote(out_buf.at[u], out.at[pl.ds(1, SLOTS), here, :], sibling))

    get_factor.wait()
    high, low = split(fac[...])
    fac_high[...] = high
    fac_low[...] = low
    add_near_lists(one)
    send_far(two, 0, 2)
    send_far(two, 1, 2)
    a2_far(one)
    a2_near(one)
    send_far(two, 0, 3)
    send_far(two, 1, 3)
    add_near_lists(two)
    a2_merge(one)
    a2_far(two)
    a3_start(one)
    a2_near(two)
    a2_merge(two)
    a3_merge(one)
    a3_end(one)
    update(one)
    a3_start(two)
    b3_far(one)
    a3_merge(two)
    b2_start(one)
    a3_end(two)
    update(two)
    b2_far(one)
    b3_far(two)
    b2_start(two)
    b1_far(one)
    b2_far(two)
    b1_near(one)
    b1_merge(one)
    b1_far(two)
    b1_near(two)
    finish(one)
    b1_merge(two)
    finish(two)
    for copy in last:
        copy.wait_recv()
    for copy in sent:
        copy.wait_send()
    for pieces in streams:
        for p in pieces:
            assert p.slots_sent == PIECE_SLOTS
            wait_all(blocks.at[:, pl.ds(0, 88), pl.ds(0, 32 * p.rows)], p.send)


def output_kernel(held, owned, returned, sems):
    copies = (
        pltpu.make_async_copy(held.at[0], owned, sems.at[0]),
        pltpu.make_async_copy(held.at[pl.ds(1, SLOTS)], returned, sems.at[1]),
    )
    for copy in copies:
        copy.start()
    for copy in copies:
        copy.wait()


def local_step(blocks, features, col_ids, row_ids, factor):
    scratch = []
    for u in range(STREAMS):
        for _, rows in PIECES[u]:
            for _, depth in PIECE_BUFFERS:
                scratch.append(pltpu.VMEM((depth, rows, LANES), F32))
    scratch += [
        pltpu.VMEM((RING, B, BPR * B), F32),
        pltpu.VMEM((FT, B, FEAT), F32),
        pltpu.VMEM((FT * B, FEAT), BF16),
        pltpu.VMEM((FT * B, FEAT), BF16),
        pltpu.VMEM((BPR + 1, B, B), F32),
        pltpu.VMEM((B, FT * B), BF16),
        pltpu.VMEM((B, FT * B), BF16),
        pltpu.VMEM((SLOTS, 2, STREAMS, TILE_ROWS, LANES), F32),
        pltpu.VMEM((48, STREAMS, TILE_ROWS, LANES), F32),
        pltpu.VMEM((SLOTS, BPR), I32),
        pltpu.VMEM((16, LANES), I32),
        pltpu.SMEM((16, LANES), I32),
        pltpu.SMEM((SLOTS,), I32),
        pltpu.VMEM((8, LANES), I32),
        pltpu.VMEM((10, 16, LANES), I32),
        pltpu.VMEM((3, 8, LANES), I32),
        pltpu.SMEM((3, 8, LANES), I32),
        pltpu.VMEM((STREAMS, 2, TILE_ROWS, LANES), F32),
        pltpu.VMEM((STREAMS, ROWS, FEAT), F32),
        pltpu.VMEM((STREAMS, SLOTS, ROWS, FEAT), F32),
        pltpu.VMEM((FEAT, FEAT), F32),
        pltpu.VMEM((FEAT, FEAT), BF16),
        pltpu.VMEM((FEAT, FEAT), BF16),
        pltpu.SemaphoreType.DMA((N_SEND,)),
        pltpu.SemaphoreType.DMA((N_RECV,)),
        pltpu.SemaphoreType.DMA((N_LOCAL,)),
    ]
    hbm = pl.BlockSpec(memory_space=pl.ANY)
    held = pl.pallas_call(
        kernel,
        in_specs=[hbm] * 5,
        out_specs=pl.BlockSpec(memory_space=pltpu.VMEM),
        out_shape=jax.ShapeDtypeStruct((1 + SLOTS, B, FEAT), F32),
        scratch_shapes=scratch,
        compiler_params=pltpu.CompilerParams(
            collective_id=0, has_side_effects=True, vmem_limit_bytes=VMEM_LIMIT
        ),
    )(blocks, features, col_ids, row_ids, factor)
    owned, returned = pl.pallas_call(
        output_kernel,
        in_specs=[pl.BlockSpec(memory_space=pltpu.VMEM)],
        out_specs=[hbm] * 2,
        out_shape=[
            jax.ShapeDtypeStruct((B, FEAT), F32),
            jax.ShapeDtypeStruct((SLOTS, B, FEAT), F32),
        ],
        scratch_shapes=[pltpu.SemaphoreType.DMA((2,))],
        compiler_params=pltpu.CompilerParams(vmem_limit_bytes=1 << 20),
    )(held)
    return owned, returned.reshape(SLOTS * B, FEAT)


def solution(mesh):
    return jax.shard_map(
        local_step,
        mesh=mesh,
        in_specs=(
            P(("gx", "gy"), None, None),
            P(("gx", "gy"), None, None),
            P(("gx", "gy"), None),
            P(("gx", "gy")),
            P(),
        ),
        out_specs=(P(("gx", "gy"), None), P(("gx", "gy"), None)),
        check_vma=False,
    )
```

```python
import functools

import jax
import jax.numpy as jnp
from jax import lax
from jax.experimental import pallas as pl
from jax.experimental.pallas import tpu as pltpu
from jax.sharding import PartitionSpec as P

MESH = pl.DeviceIdType.MESH
F32 = jnp.float32
BF16 = jnp.bfloat16
I32 = jnp.int32

B = 128
FEAT = 512
SLOTS = 6
BPR = 32
FT = 16
HALF = B // 2
STREAMS = 4
ROWS = HALF // STREAMS
LANES = 128
GROUPS = FEAT // LANES
TILE_ROWS = ROWS * GROUPS
SHIFT = {"z": 5, "y": 3, "x": 1}
ORDERS = ("zyx", "yxz", "xzy")
PIECES = (
    ((0, 24), (24, 24), (48, 16)),
    ((0, 24), (24, 16), (40, 24)),
    ((0, 16), (16, 24), (40, 24)),
    ((0, 24), (24, 24), (48, 16)),
)
CHUNKS = ((0, 1), (1, 1), (2, 2), (4, 2))
FAR_UP = ((0, 0), (1, 0), (0, 1), (1, 1), (0, 3))
FAR_DOWN = ((0, 2), (1, 2), (1, 3))


def split(value):
    high = value.astype(BF16)
    return high, (value - high.astype(F32)).astype(BF16)


def product(left_high, left_low, right_high, right_low):
    dot = functools.partial(jnp.dot, preferred_element_type=F32)
    return dot(left_high, right_high) + (dot(left_high, right_low) + dot(left_low, right_high))


PIECE_BUFFERS = (
    ("sums", 49),
    ("a2_far_up", 4),
    ("a2_far_down", 4),
    ("a2_got_far_up", 4),
    ("a2_got_far_down", 4),
    ("a2_up", 8),
    ("a2_down", 8),
    ("a2_got", 16),
    ("quarter", 8),
    ("a3_got_far", 2),
    ("a3_up", 1),
    ("a3_down", 1),
    ("a3_got", 4),
    ("dense", 33),
    ("b1_got_far_up", 6),
    ("b1_got_far_down", 6),
    ("b1_got", 24),
)
STREAM_SLOTS = 36 + 24 + 6 + 6 + 24 + 36
N_SEND = 32
N_RECV = 110
N_LOCAL = 14
RING = 4
VMEM_LIMIT = 58 << 20

(
    MAKE, GIVE, SEND, PASS_ON, TABLES, NEAR, A2_FAR, A2_NEAR, A2_MERGE, A3,
    A3_MERGE, UPDATE, B3_FAR, B2, B2_FAR, B1_FAR, B1_NEAR, B1_MERGE, FINISH,
) = range(19)
ORDER = (
    (MAKE, 0), (GIVE, 0), (SEND, 0, 0, 0), (SEND, 2, 0, 0), (SEND, 1, 0, 0), (SEND, 3, 0, 0),
    (MAKE, 1), (GIVE, 1), (SEND, 0, 0, 1), (SEND, 2, 1, 0), (SEND, 3, 1, 0), (MAKE, 2),
    (SEND, 0, 1, 1), (SEND, 2, 1, 1), (MAKE, 3), (GIVE, 2), (SEND, 2, 0, 2), (SEND, 0, 0, 2),
    (SEND, 1, 0, 2), (MAKE, 4), (SEND, 3, 1, 2), (SEND, 1, 1, 2), (SEND, 2, 1, 2), (MAKE, 5),
    (GIVE, 3), (SEND, 1, 0, 1), (SEND, 1, 1, 1), (PASS_ON, 0, 1, 1), (SEND, 1, 1, 0),
    (SEND, 0, 1, 0), (SEND, 3, 0, 1), (SEND, 0, 1, 2), (SEND, 0, 0, 3), (SEND, 1, 0, 3),
    (PASS_ON, 3, 0, 0), (PASS_ON, 0, 0, 1), (PASS_ON, 2, 0, 0), (PASS_ON, 2, 1, 0),
    (PASS_ON, 3, 1, 0), (TABLES,), (SEND, 0, 1, 3), (PASS_ON, 1, 1, 2), (PASS_ON, 2, 0, 2),
    (PASS_ON, 3, 1, 2), (SEND, 1, 1, 3), (PASS_ON, 0, 0, 2), (PASS_ON, 0, 0, 0), (PASS_ON, 2, 1, 1),
    (PASS_ON, 1, 0, 2), (PASS_ON, 1, 0, 0), (PASS_ON, 2, 1, 2), (PASS_ON, 1, 0, 1),
    (PASS_ON, 1, 1, 1), (PASS_ON, 1, 1, 0), (PASS_ON, 0, 1, 0), (PASS_ON, 3, 0, 1),
    (PASS_ON, 0, 1, 2), (PASS_ON, 0, 0, 3), (PASS_ON, 1, 0, 3), (PASS_ON, 0, 1, 3), (SEND, 2, 1, 3),
    (SEND, 3, 0, 2), (SEND, 2, 0, 1), (NEAR, 0), (SEND, 2, 0, 3), (PASS_ON, 1, 1, 3), (NEAR, 1),
    (SEND, 3, 0, 3), (SEND, 3, 1, 3), (SEND, 3, 1, 1), (A2_FAR, 0), (PASS_ON, 2, 1, 3),
    (A2_NEAR, 0), (PASS_ON, 3, 0, 2), (PASS_ON, 2, 0, 1), (PASS_ON, 2, 0, 3), (NEAR, 2),
    (A2_FAR, 1), (PASS_ON, 3, 0, 3), (PASS_ON, 3, 1, 3), (PASS_ON, 3, 1, 1), (NEAR, 3),
    (A2_MERGE, 0), (A2_NEAR, 1), (A2_FAR, 2), (A2_NEAR, 2), (A2_MERGE, 1), (A3, 0), (A2_FAR, 3),
    (A2_MERGE, 2), (A2_NEAR, 3), (A3, 1), (A3_MERGE, 0), (A2_MERGE, 3), (A3, 2), (A3_MERGE, 1),
    (UPDATE, 0), (A3, 3), (A3_MERGE, 2), (UPDATE, 1), (B3_FAR, 0), (A3_MERGE, 3), (UPDATE, 2),
    (B3_FAR, 1), (B2, 0), (UPDATE, 3), (B3_FAR, 2), (B2, 1), (B2_FAR, 0), (B3_FAR, 3), (B2, 2),
    (B2_FAR, 1), (B1_FAR, 0), (B2, 3), (B2_FAR, 2), (B1_FAR, 1), (B1_NEAR, 1), (B2_FAR, 3),
    (B1_NEAR, 0), (B1_MERGE, 0), (B1_MERGE, 1), (B1_FAR, 3), (B1_FAR, 2), (B1_NEAR, 2), (FINISH, 0),
    (FINISH, 1), (B1_NEAR, 3), (B1_MERGE, 3), (B1_MERGE, 2), (FINISH, 3), (FINISH, 2),
)


class Piece:
    pass


class Stream:
    pass


def kernel(blocks, features, col_ids, row_ids, factor, out, *scratch):
    scratch = list(scratch)
    streams = []
    for u in range(STREAMS):
        stream = Stream()
        stream.number, stream.pieces, stream.elements_sent = u, [], 0
        for number, (start, rows) in enumerate(PIECES[u]):
            p = Piece()
            p.number, p.start, p.rows = number, start, rows
            for name, _ in PIECE_BUFFERS:
                setattr(p, name, scratch.pop(0))
            p.b1_far_up, p.b1_far_down = p.sums.at[pl.ds(1, 6)], p.sums.at[pl.ds(7, 6)]
            p.b1_up, p.b1_down = p.sums.at[pl.ds(13, 12)], p.sums.at[pl.ds(25, 12)]
            stream.pieces.append(p)
        streams.append(stream)
    (
        blk, feat, f_high, f_low, chain, a_high, a_low, part, entries, cols, col_v, col_tab, ids,
        tile, lab, tab_v, tab, x_buf, y_buf, out_buf, fac, fac_high, fac_low,
        send_sem, recv_sem, local_sem,
    ) = scratch

    z = lax.axis_index("gx")
    gy = lax.axis_index("gy")
    core = gy % 2
    at = {"z": z, "y": gy // 8, "x": (gy // 2) % 4}

    def neighbour(axis, step):
        to = dict(at)
        to[axis] = (at[axis] + step) % 4
        return (to["z"], to["y"] * 8 + to["x"] * 2 + core)

    sibling = (z, gy - core + (1 - core))
    counts = {"send": 0, "recv": 0, "local": 0}
    sent = []

    def take(kind, limit):
        n = counts[kind]
        counts[kind] += 1
        assert n < limit
        return n

    def arrival():
        return recv_sem.at[take("recv", N_RECV)]

    for stream in streams:
        stream.send = send_sem.at[take("send", N_SEND)]
        for p in stream.pieces:
            p.stream = stream
            p.ways = [(neighbour(axis, 1), neighbour(axis, 3)) for axis in ORDERS[p.number]]

    def remote(source, target, device, stream=None, recv=None):
        copy = pltpu.make_async_remote_copy(
            src_ref=source,
            dst_ref=target,
            send_sem=send_sem.at[take("send", N_SEND)] if stream is None else stream.send,
            recv_sem=arrival() if recv is None else recv,
            device_id=device,
            device_id_type=MESH,
        )
        copy.start()
        if stream is None:
            sent.append(copy)
        else:
            elements = 1
            for size in source.shape:
                elements *= size
            stream.elements_sent += elements
        return copy

    def wait_slots(stream, slots, sem):
        ref = entries.at[pl.ds(0, slots), stream.number]
        pltpu.make_async_copy(ref, ref, sem).wait()

    def local(source, target):
        copy = pltpu.make_async_copy(source, target, local_sem.at[take("local", N_LOCAL)])
        copy.start()
        return copy

    barrier = pltpu.get_barrier_semaphore()
    greeted = [sibling] + [neighbour(axis, step) for axis in "zyx" for step in (1, 3)]
    for device in greeted:
        pl.semaphore_signal(barrier, inc=1, device_id=device, device_id_type=MESH)
    get_cols = local(col_ids, cols)
    get_ids = local(row_ids, ids)
    get_feat = [local(features.at[pl.ds(0, 8)], feat.at[pl.ds(0, 8)])]
    get_blk = {0: local(blocks.at[0], blk.at[0])}
    get_feat.append(local(features.at[pl.ds(8, 8)], feat.at[pl.ds(8, 8)]))
    for k in range(1, RING):
        get_blk[k] = local(blocks.at[k], blk.at[k])
    get_factor = local(factor, fac)

    get_cols.wait()
    row = lax.broadcasted_iota(I32, (BPR, BPR), 0)
    lane = lax.broadcasted_iota(I32, (BPR, BPR), 1)
    for k in range(SLOTS):
        across = jnp.broadcast_to(cols[pl.ds(k, 1), :], (BPR, BPR))
        down = jnp.sum(jnp.where(row == lane, across, 0), axis=1, keepdims=True)
        col_v[pl.ds(2 * k, 1), pl.ds(0, BPR)] = jnp.max(
            jnp.where(jnp.logical_and(down == across, row < lane), row + 1, 0), axis=0, keepdims=True
        )
        col_v[pl.ds(2 * k + 1, 1), pl.ds(0, BPR)] = jnp.max(
            jnp.where(down == lane, row + 1, 0), axis=0, keepdims=True
        )
    get_ids.wait()
    line = lax.broadcasted_iota(I32, (8, LANES), 0)
    names = jnp.full((8, LANES), -1, I32)
    for s in range(SLOTS):
        names = jnp.where(line == s, ids[s], names)
    tile[...] = names
    chain[0] = jnp.zeros((B, B), F32)
    for stream in streams:
        for p in stream.pieces:
            p.sums[0] = jnp.zeros((p.rows, LANES), F32)
            p.dense[0] = jnp.zeros((p.rows, LANES), F32)

    get_col_tab = local(col_v, col_tab)

    def convert(first):
        def body(t, carry):
            high, low = split(feat[t])
            f_high[pl.ds(pl.multiple_of(t * B, B), B), :] = high
            f_low[pl.ds(pl.multiple_of(t * B, B), B), :] = low
            return carry

        lax.fori_loop(first, first + 8, body, 0)

    def gather_sums(k):
        get_blk[k].wait()
        held = blk.at[k % RING]

        for j in range(BPR):
            chain[j + 1] = held[:, pl.ds(j * B, B)] + chain[col_tab[2 * k, j]]
        for t in range(FT):
            high, low = split(chain[col_tab[2 * k + 1, t]])
            a_high[:, pl.ds(t * B, B)] = high
            a_low[:, pl.ds(t * B, B)] = low
        if k + RING < SLOTS:
            get_blk[k + RING] = local(blocks.at[k + RING], blk.at[k % RING])

    def make(k):
        gather_sums(k)
        result = product(a_high[...], a_low[...], f_high[...], f_low[...])
        for half in range(2):
            for u in range(STREAMS):
                first = half * HALF + u * ROWS
                for g in range(GROUPS):
                    part[k, half, u, pl.ds(g * ROWS, ROWS), :] = result[
                        first : first + ROWS, g * LANES : (g + 1) * LANES
                    ]

    give_part = {}

    def place_of(half, chunk):
        return half * SLOTS + CHUNKS[chunk][0]

    def send_part(chunk):
        first, number = CHUNKS[chunk]
        give_part[chunk] = remote(
            part.at[pl.ds(first, number), 1 - core],
            entries.at[pl.ds(place_of(1, chunk), number)],
            sibling,
        )

    WAYS = {"up": 1, "down": 2}

    def send_list(stream, half, chunk):
        first, number = CHUNKS[chunk]
        if half == 1 and chunk not in arrived:
            arrived.add(chunk)
            give_part[chunk].wait_recv()
        stream.lists[half, chunk] = arrival()
        for p in stream.pieces:
            here = pl.ds(p.start, p.rows)
            if half == 0:
                source = part.at[pl.ds(first, number), core, stream.number, here]
            else:
                source = entries.at[pl.ds(place_of(1, chunk), number), stream.number, here]
            for name, far, device in zip(("up", "down"), (FAR_UP, FAR_DOWN), p.ways[0]):
                target = entries.at[
                    pl.ds(WAYS[name] * 12 + place_of(half, chunk), number), stream.number, here
                ]
                recv = stream.lists[half, chunk] if (half, chunk) in far else stream.list_recv
                remote(source, target, device, stream, recv)

    def send_far(stream, half, chunk):
        up = (half, chunk) in FAR_UP
        number = CHUNKS[chunk][1]
        wait_slots(stream, number, stream.lists[half, chunk])
        for p in stream.pieces:
            here = pl.ds(p.start, p.rows)
            remote(
                entries.at[
                    pl.ds(WAYS["up" if up else "down"] * 12 + place_of(half, chunk), number),
                    stream.number,
                    here,
                ],
                entries.at[pl.ds(36 + place_of(half, chunk), number), stream.number, here],
                p.ways[0][0 if up else 1],
                stream,
                stream.far_recv,
            )

    arrived = set()
    for stream in streams:
        stream.lists = {}
        stream.list_recv, stream.far_recv = arrival(), arrival()

    def make_table(j):
        lab_down[j].wait_recv()
        lab_far[j].wait_recv()
        first, second, third = ORDERS[j]
        seen = jnp.concatenate([lab[0], lab[1 + 3 * j], lab[2 + 3 * j], lab[3 + 3 * j]], axis=0)
        row = lax.broadcasted_iota(I32, (64, LANES), 0)
        lane = lax.broadcasted_iota(I32, (64, LANES), 1)
        place_of_row = (row >> 4) * 12 + ((row >> 3) & 1) * 6 + (row & 7) + 1
        wanted = jnp.sum(jnp.where(row == lane, seen, 0), axis=0, keepdims=True)
        previous = jnp.max(
            jnp.where(jnp.logical_and(seen == wanted, row < lane), place_of_row, 0),
            axis=0,
            keepdims=True,
        )

        def step_of(order):
            return jnp.where(order == 1, 3, jnp.where(order == 2, 1, jnp.where(order == 3, 2, 0)))

        def order_of(step):
            return jnp.where(step == 0, 0, jnp.where(step == 3, 1, step + 1))

        named = (
            (at[first] << SHIFT[first])
            + (((at[second] + step_of((lane >> 3) & 3)) & 3) << SHIFT[second])
            + (((at[third] + step_of((lane >> 1) & 3)) & 3) << SHIFT[third])
            + (lane & 1)
        )
        last = jnp.max(jnp.where(seen == named, place_of_row, 0), axis=0, keepdims=True)
        place = (
            1
            + order_of((((wanted >> SHIFT[second]) & 3) - at[second]) & 3) * 8
            + order_of((((wanted >> SHIFT[third]) & 3) - at[third]) & 3) * 2
            + (wanted & 1)
        )
        place = jnp.where(((wanted >> SHIFT[first]) & 3) == at[first], place, 0)
        tab_v[j] = jnp.where(line == 0, previous, jnp.where(line == 1, last, place))

    def add_list(stream, order):
        for h in range(2):
            for slot in range(SLOTS):
                place = order * 12 + h * 6 + slot
                for p in stream.pieces:
                    here = pl.ds(p.start, p.rows)
                    if order == 0 and h == 0:
                        value = part[slot, core, stream.number, here]
                    else:
                        value = entries[place, stream.number, here]
                    p.sums[place + 1] = value + p.sums[tab[p.number, 0, order * 16 + h * 8 + slot]]

    def near_lists(stream):
        add_list(stream, 0)
        wait_slots(stream, 12, stream.list_recv)
        add_list(stream, 1)
        add_list(stream, 2)

    def pick(p, r):
        return p.sums[tab[p.number, 1, r]]

    def loop(stream, n, body):
        def step(m, carry):
            for p in stream.pieces:
                body(p, m)
            return carry

        lax.fori_loop(0, n, step, 0)

    def a2_far(stream):
        wait_slots(stream, 12, stream.far_recv)
        add_list(stream, 3)

        def body(p, m):
            p.a2_far_up[m] = pick(p, 24 + m)
            p.a2_far_down[m] = pick(p, 28 + m)

        loop(stream, 4, body)
        stream.a2_far, stream.a2_recv = arrival(), arrival()
        for p in stream.pieces:
            up, down = p.ways[1]
            remote(p.a2_far_up, p.a2_got_far_up, up, stream, stream.a2_far)
            remote(p.a2_far_down, p.a2_got_far_down, down, stream, stream.a2_far)

    def a2_near(stream):
        def body(p, m):
            p.a2_up[m + 4] = pick(p, 20 + m)
            p.a2_down[m] = pick(p, 8 + m)

        loop(stream, 4, body)
        for p in stream.pieces:
            up, down = p.ways[1]
            remote(p.a2_up.at[pl.ds(4, 4)], p.a2_got.at[pl.ds(4, 4)], up, stream, stream.a2_recv)
            remote(p.a2_down.at[pl.ds(0, 4)], p.a2_got.at[pl.ds(8, 4)], down, stream, stream.a2_recv)

    def a2_merge(stream):
        wait_slots(stream, 8, stream.a2_far)

        def body(p, m):
            p.a2_up[m] = p.a2_got_far_up[m] + pick(p, 16 + m)
            p.a2_down[m + 4] = p.a2_got_far_down[m] + pick(p, 12 + m)

        loop(stream, 4, body)
        for p in stream.pieces:
            up, down = p.ways[1]
            remote(p.a2_up.at[pl.ds(0, 4)], p.a2_got.at[pl.ds(0, 4)], up, stream, stream.a2_recv)
            remote(p.a2_down.at[pl.ds(4, 4)], p.a2_got.at[pl.ds(12, 4)], down, stream, stream.a2_recv)

    def a3_start(stream):
        wait_slots(stream, 16, stream.a2_recv)

        def body(p, m):
            p.quarter[m] = pick(p, m) + (p.a2_got[m] + p.a2_got[8 + m])

        loop(stream, 8, body)
        stream.a3_far, stream.a3_recv = arrival(), arrival()
        for p in stream.pieces:
            up, down = p.ways[2]
            remote(p.quarter.at[6], p.a3_got_far.at[0], up, stream, stream.a3_far)
            remote(p.quarter.at[7], p.a3_got_far.at[1], down, stream, stream.a3_far)
        for p in stream.pieces:
            up, down = p.ways[2]
            remote(p.quarter.at[5], p.a3_got.at[1], up, stream, stream.a3_recv)
            remote(p.quarter.at[2], p.a3_got.at[2], down, stream, stream.a3_recv)

    def a3_merge(stream):
        wait_slots(stream, 2, stream.a3_far)
        for p in stream.pieces:
            p.a3_up[0] = p.quarter[4] + p.a3_got_far[0]
            p.a3_down[0] = p.quarter[3] + p.a3_got_far[1]
        for p in stream.pieces:
            up, down = p.ways[2]
            remote(p.a3_up.at[0], p.a3_got.at[0], up, stream, stream.a3_recv)
            remote(p.a3_down.at[0], p.a3_got.at[3], down, stream, stream.a3_recv)

    last = []

    def update(stream):
        u = stream.number
        wait_slots(stream, 4, stream.a3_recv)
        for p in stream.pieces:
            for b in range(2):
                x_buf[u, b, pl.ds(p.start, p.rows), :] = jnp.tanh(
                    p.quarter[b] + (p.a3_got[b] + p.a3_got[2 + b])
                )
        x = jnp.concatenate(
            [
                jnp.concatenate(
                    [x_buf[u, b, pl.ds(g * ROWS, ROWS), :] for g in range(GROUPS)], axis=1
                )
                for b in range(2)
            ],
            axis=0,
        )
        x_high, x_low = split(x)
        y = product(x_high, x_low, fac_high[...], fac_low[...])
        for b in range(2):
            rows_y = y[b * ROWS : (b + 1) * ROWS]
            flat = jnp.concatenate(
                [rows_y[:, g * LANES : (g + 1) * LANES] for g in range(GROUPS)], axis=0
            )
            for p in stream.pieces:
                p.dense[1 + b] = flat[p.start : p.start + p.rows]
        stream.b3_far, stream.b3_recv = arrival(), arrival()
        for p in stream.pieces:
            d, (up, down) = p.dense, p.ways[2]
            remote(d.at[1], d.at[3], up, stream, stream.b3_far)
            remote(d.at[2], d.at[6], down, stream, stream.b3_far)
        for p in stream.pieces:
            d, (up, down) = p.dense, p.ways[2]
            remote(d.at[2], d.at[4], up, stream, stream.b3_recv)
            remote(d.at[1], d.at[5], down, stream, stream.b3_recv)
        here = pl.ds(pl.multiple_of(core * HALF + u * ROWS, ROWS), ROWS)
        out[0, here, :] = jnp.where(core == 0, y[:ROWS], y[ROWS:])
        y_buf[u] = jnp.where(core == 0, y[ROWS:], y[:ROWS])
        last.append(remote(y_buf.at[u], out.at[0, here, :], sibling))

    def b3_far(stream):
        wait_slots(stream, 2, stream.b3_far)
        for p in stream.pieces:
            d, (up, down) = p.dense, p.ways[2]
            remote(d.at[3], d.at[7], up, stream, stream.b3_recv)
            remote(d.at[6], d.at[8], down, stream, stream.b3_recv)

    def b2_start(stream):
        wait_slots(stream, 4, stream.b3_recv)
        stream.b2_far, stream.b2_recv = arrival(), arrival()
        for p in stream.pieces:
            d, (up, down) = p.dense, p.ways[1]
            remote(d.at[pl.ds(1, 4)], d.at[pl.ds(9, 4)], up, stream, stream.b2_far)
            remote(d.at[pl.ds(5, 4)], d.at[pl.ds(21, 4)], down, stream, stream.b2_far)
        for p in stream.pieces:
            d, (up, down) = p.dense, p.ways[1]
            remote(d.at[pl.ds(5, 4)], d.at[pl.ds(13, 4)], up, stream, stream.b2_recv)
            remote(d.at[pl.ds(1, 4)], d.at[pl.ds(17, 4)], down, stream, stream.b2_recv)

    def b2_far(stream):
        wait_slots(stream, 8, stream.b2_far)
        for p in stream.pieces:
            d, (up, down) = p.dense, p.ways[1]
            remote(d.at[pl.ds(9, 4)], d.at[pl.ds(25, 4)], up, stream, stream.b2_recv)
            remote(d.at[pl.ds(21, 4)], d.at[pl.ds(29, 4)], down, stream, stream.b2_recv)

    def answer(p, i):
        return p.dense[tab[p.number, 2, i]]

    def b1_far(stream):
        wait_slots(stream, 16, stream.b2_recv)

        def body(p, h):
            for s in range(3):
                p.b1_far_up[h * 3 + s] = answer(p, 48 + h * 8 + s)
                p.b1_far_down[h * 3 + s] = answer(p, 51 + h * 8 + s)

        loop(stream, 2, body)
        stream.b1_far, stream.b1_recv = arrival(), arrival()
        for p in stream.pieces:
            up, down = p.ways[0]
            remote(p.b1_far_up, p.b1_got_far_up, up, stream, stream.b1_far)
            remote(p.b1_far_down, p.b1_got_far_down, down, stream, stream.b1_far)

    def b1_near(stream):
        def body(p, h):
            for s in range(3):
                p.b1_up[6 + h * 3 + s] = answer(p, 35 + h * 8 + s)
                p.b1_down[h * 3 + s] = answer(p, 16 + h * 8 + s)

        loop(stream, 2, body)
        for p in stream.pieces:
            up, down = p.ways[0]
            remote(p.b1_up.at[pl.ds(6, 6)], p.b1_got.at[pl.ds(6, 6)], up, stream, stream.b1_recv)
            remote(p.b1_down.at[pl.ds(0, 6)], p.b1_got.at[pl.ds(12, 6)], down, stream, stream.b1_recv)

    def b1_merge(stream):
        wait_slots(stream, 12, stream.b1_far)

        def body(p, h):
            for s in range(3):
                p.b1_up[h * 3 + s] = p.b1_got_far_up[h * 3 + s] + answer(p, 32 + h * 8 + s)
                p.b1_down[6 + h * 3 + s] = p.b1_got_far_down[h * 3 + s] + answer(p, 19 + h * 8 + s)

        loop(stream, 2, body)
        for p in stream.pieces:
            up, down = p.ways[0]
            remote(p.b1_up.at[pl.ds(0, 6)], p.b1_got.at[pl.ds(0, 6)], up, stream, stream.b1_recv)
            remote(p.b1_down.at[pl.ds(6, 6)], p.b1_got.at[pl.ds(18, 6)], down, stream, stream.b1_recv)

    def finish(stream):
        u = stream.number
        first = core * HALF + u * ROWS
        wait_slots(stream, 24, stream.b1_recv)

        def body(p, n):
            t, s = n // 3, n % 3
            for h in (1, 0):
                q = t * 6 + h * 3 + s
                value = answer(p, h * 8 + n) + (p.b1_got[q] + p.b1_got[12 + q])
                done = 0
                while done < p.rows:
                    g, r = divmod(p.start + done, ROWS)
                    size = min(ROWS - r, p.rows - done)
                    across = pl.ds(g * LANES, LANES)
                    if h == 0:
                        rows = pl.ds(pl.multiple_of(first + r, 8), size)
                        out[1 + n, rows, across] = value[done : done + size]
                    else:
                        out_buf[u, n, pl.ds(r, size), across] = value[done : done + size]
                    done += size

        loop(stream, SLOTS, body)
        here = pl.ds(pl.multiple_of(first, ROWS), ROWS)
        last.append(remote(out_buf.at[u], out.at[pl.ds(1, SLOTS), here, :], sibling))

    get_feat[0].wait()
    convert(0)
    get_feat[1].wait()
    convert(8)
    get_col_tab.wait()
    lab_up, lab_down, lab_far = {}, {}, {}
    waiting = {}

    def product_block(k):
        make(k)
        if k == 0:
            pl.semaphore_wait(barrier, len(greeted))
            waiting["give"] = remote(tile, lab.at[0, pl.ds(8, 8)], sibling)
            waiting["keep"] = local(tile, lab.at[0, pl.ds(0, 8)])
        if k == 1:
            waiting["keep"].wait()
            waiting["give"].wait_recv()
            for j in range(3):
                lab_up[j] = remote(lab.at[0], lab.at[1 + 3 * j], neighbour(ORDERS[j][0], 1))
                lab_down[j] = remote(lab.at[0], lab.at[2 + 3 * j], neighbour(ORDERS[j][0], 3))
        if k == 4:
            for j in range(3):
                lab_up[j].wait_recv()
                lab_far[j] = remote(
                    lab.at[1 + 3 * j], lab.at[3 + 3 * j], neighbour(ORDERS[j][0], 1)
                )

    def tables():
        for j in range(3):
            make_table(j)
        get_factor.wait()
        high, low = split(fac[...])
        fac_high[...] = high
        fac_low[...] = low
        local(tab_v, tab).wait()

    blocks_of = {
        MAKE: product_block, GIVE: send_part, SEND: send_list, PASS_ON: send_far, TABLES: tables,
        NEAR: near_lists, A2_FAR: a2_far, A2_NEAR: a2_near, A2_MERGE: a2_merge, A3: a3_start,
        A3_MERGE: a3_merge, UPDATE: update, B3_FAR: b3_far, B2: b2_start, B2_FAR: b2_far,
        B1_FAR: b1_far, B1_NEAR: b1_near, B1_MERGE: b1_merge, FINISH: finish,
    }
    for kind, *numbers in ORDER:
        if kind in (MAKE, GIVE, TABLES):
            blocks_of[kind](*numbers)
        else:
            blocks_of[kind](streams[numbers[0]], *numbers[1:])
    for copy in last:
        copy.wait_recv()
    for copy in sent:
        copy.wait_send()
    for stream in streams:
        assert stream.elements_sent == STREAM_SLOTS * TILE_ROWS * LANES
        ref = blocks.at[:, pl.ds(0, 88), pl.ds(0, 32 * TILE_ROWS)]
        pltpu.make_async_copy(ref, ref, stream.send).wait()


def output_kernel(held, owned, returned, sems):
    copies = (
        pltpu.make_async_copy(held.at[0], owned, sems.at[0]),
        pltpu.make_async_copy(held.at[pl.ds(1, SLOTS)], returned, sems.at[1]),
    )
    for copy in copies:
        copy.start()
    for copy in copies:
        copy.wait()


def local_step(blocks, features, col_ids, row_ids, factor):
    scratch = []
    for u in range(STREAMS):
        for _, rows in PIECES[u]:
            for _, depth in PIECE_BUFFERS:
                scratch.append(pltpu.VMEM((depth, rows, LANES), F32))
    scratch += [
        pltpu.VMEM((RING, B, BPR * B), F32),
        pltpu.VMEM((FT, B, FEAT), F32),
        pltpu.VMEM((FT * B, FEAT), BF16),
        pltpu.VMEM((FT * B, FEAT), BF16),
        pltpu.VMEM((BPR + 1, B, B), F32),
        pltpu.VMEM((B, FT * B), BF16),
        pltpu.VMEM((B, FT * B), BF16),
        pltpu.VMEM((SLOTS, 2, STREAMS, TILE_ROWS, LANES), F32),
        pltpu.VMEM((48, STREAMS, TILE_ROWS, LANES), F32),
        pltpu.VMEM((SLOTS, BPR), I32),
        pltpu.VMEM((16, LANES), I32),
        pltpu.SMEM((16, LANES), I32),
        pltpu.SMEM((SLOTS,), I32),
        pltpu.VMEM((8, LANES), I32),
        pltpu.VMEM((10, 16, LANES), I32),
        pltpu.VMEM((3, 8, LANES), I32),
        pltpu.SMEM((3, 8, LANES), I32),
        pltpu.VMEM((STREAMS, 2, TILE_ROWS, LANES), F32),
        pltpu.VMEM((STREAMS, ROWS, FEAT), F32),
        pltpu.VMEM((STREAMS, SLOTS, ROWS, FEAT), F32),
        pltpu.VMEM((FEAT, FEAT), F32),
        pltpu.VMEM((FEAT, FEAT), BF16),
        pltpu.VMEM((FEAT, FEAT), BF16),
        pltpu.SemaphoreType.DMA((N_SEND,)),
        pltpu.SemaphoreType.DMA((N_RECV,)),
        pltpu.SemaphoreType.DMA((N_LOCAL,)),
    ]
    hbm = pl.BlockSpec(memory_space=pl.ANY)
    held = pl.pallas_call(
        kernel,
        in_specs=[hbm] * 5,
        out_specs=pl.BlockSpec(memory_space=pltpu.VMEM),
        out_shape=pltpu.VMEM((1 + SLOTS, B, FEAT), F32),
        scratch_shapes=scratch,
        compiler_params=pltpu.CompilerParams(
            collective_id=0, has_side_effects=True, vmem_limit_bytes=VMEM_LIMIT
        ),
    )(blocks, features, col_ids, row_ids, factor)
    owned, returned = pl.pallas_call(
        output_kernel,
        in_specs=[pl.BlockSpec(memory_space=pltpu.VMEM)],
        out_specs=[hbm] * 2,
        out_shape=[
            jax.ShapeDtypeStruct((B, FEAT), F32),
            jax.ShapeDtypeStruct((SLOTS, B, FEAT), F32),
        ],
        scratch_shapes=[pltpu.SemaphoreType.DMA((2,))],
        compiler_params=pltpu.CompilerParams(vmem_limit_bytes=1 << 20),
    )(held)
    return owned, returned.reshape(SLOTS * B, FEAT)


def solution(mesh):
    return jax.shard_map(
        local_step,
        mesh=mesh,
        in_specs=(
            P(("gx", "gy"), None, None),
            P(("gx", "gy"), None, None),
            P(("gx", "gy"), None),
            P(("gx", "gy")),
            P(),
        ),
        out_specs=(P(("gx", "gy"), None), P(("gx", "gy"), None)),
        check_vma=False,
    )
```

```python
import functools

import jax
import jax.numpy as jnp
from jax import lax
from jax.experimental import pallas as pl
from jax.experimental.pallas import tpu as pltpu
from jax.sharding import PartitionSpec as P

MESH = pl.DeviceIdType.MESH
F32 = jnp.float32
BF16 = jnp.bfloat16
I32 = jnp.int32

B = 128
FEAT = 512
SLOTS = 6
BPR = 32
FT = 16
HALF = B // 2
STREAMS = 4
ROWS = HALF // STREAMS
LANES = 128
GROUPS = FEAT // LANES
TILE_ROWS = ROWS * GROUPS
SHIFT = {"z": 5, "y": 3, "x": 1}
ORDERS = ("zyx", "yxz", "xzy")
PIECES = (
    ((0, 24), (24, 24), (48, 16)),
    ((0, 24), (24, 16), (40, 24)),
    ((0, 16), (16, 24), (40, 24)),
    ((0, 24), (24, 24), (48, 16)),
)
CHUNKS = ((0, 1), (1, 1), (2, 2), (4, 2))
FAR_UP = ((0, 0), (1, 0), (0, 1), (1, 1), (0, 3))
FAR_DOWN = ((0, 2), (1, 2), (1, 3))


def split(value):
    high = value.astype(BF16)
    return high, (value - high.astype(F32)).astype(BF16)


def product(left_high, left_low, right_high, right_low):
    dot = functools.partial(jnp.dot, preferred_element_type=F32)
    return dot(left_high, right_high) + (dot(left_high, right_low) + dot(left_low, right_high))


PIECE_BUFFERS = (
    ("sums", 49),
    ("a2_far_up", 4),
    ("a2_far_down", 4),
    ("a2_got_far_up", 4),
    ("a2_got_far_down", 4),
    ("a2_up", 8),
    ("a2_down", 8),
    ("a2_got", 16),
    ("quarter", 8),
    ("a3_got_far", 2),
    ("a3_up", 1),
    ("a3_down", 1),
    ("a3_got", 4),
    ("dense", 33),
    ("b1_got_far_up", 6),
    ("b1_got_far_down", 6),
    ("b1_got", 24),
)
STREAM_SLOTS = 36 + 24 + 6 + 6 + 24 + 36
N_SEND = 36
N_RECV = 110
N_LOCAL = 16
RING = 4
VMEM_LIMIT = 58 << 20

(
    MAKE, GIVE, SEND, PASS_ON, TABLES, NEAR, A2_FAR, A2_NEAR, A2_MERGE, A3,
    A3_MERGE, UPDATE, B3_FAR, B2, B2_FAR, B1_FAR, B1_NEAR, B1_MERGE, FINISH,
) = range(19)
ORDER = (
    (MAKE, 0), (GIVE, 0), (SEND, 0, 0, 0), (SEND, 1, 0, 0), (MAKE, 1), (GIVE, 1), (SEND, 2, 0, 0),
    (SEND, 2, 1, 0), (SEND, 2, 0, 1), (SEND, 3, 0, 0), (SEND, 0, 1, 0), (SEND, 1, 1, 0),
    (SEND, 3, 0, 1), (MAKE, 2), (SEND, 1, 0, 1), (SEND, 3, 1, 1), (SEND, 0, 1, 1), (SEND, 3, 1, 0),
    (SEND, 0, 0, 1), (SEND, 1, 1, 1), (MAKE, 3), (GIVE, 2), (SEND, 2, 0, 2), (SEND, 1, 0, 2),
    (SEND, 0, 0, 2), (SEND, 2, 1, 1), (SEND, 3, 0, 2), (MAKE, 4), (SEND, 3, 1, 2), (SEND, 2, 1, 2),
    (MAKE, 5), (GIVE, 3), (SEND, 3, 0, 3), (PASS_ON, 3, 1, 1), (PASS_ON, 3, 0, 0), (SEND, 2, 0, 3),
    (SEND, 3, 1, 3), (PASS_ON, 1, 0, 2), (PASS_ON, 2, 1, 0), (SEND, 1, 1, 2), (PASS_ON, 3, 0, 1),
    (SEND, 1, 1, 3), (SEND, 2, 1, 3), (SEND, 0, 1, 3), (PASS_ON, 3, 1, 0), (TABLES,),
    (PASS_ON, 2, 0, 0), (PASS_ON, 3, 0, 2), (PASS_ON, 3, 1, 2), (PASS_ON, 3, 0, 3),
    (PASS_ON, 1, 1, 1), (PASS_ON, 1, 0, 1), (PASS_ON, 3, 1, 3), (PASS_ON, 1, 0, 0),
    (PASS_ON, 2, 0, 2), (SEND, 1, 0, 3), (PASS_ON, 2, 1, 1), (PASS_ON, 2, 1, 2), (PASS_ON, 0, 0, 2),
    (NEAR, 3), (PASS_ON, 0, 1, 0), (PASS_ON, 2, 0, 3), (PASS_ON, 2, 0, 1), (PASS_ON, 2, 1, 3),
    (PASS_ON, 1, 1, 2), (SEND, 0, 0, 3), (PASS_ON, 1, 1, 0), (SEND, 0, 1, 2), (A2_FAR, 3),
    (PASS_ON, 1, 1, 3), (PASS_ON, 1, 0, 3), (PASS_ON, 0, 1, 3), (PASS_ON, 0, 0, 0), (A2_NEAR, 3),
    (NEAR, 2), (PASS_ON, 0, 1, 1), (A2_FAR, 2), (PASS_ON, 0, 1, 2), (PASS_ON, 0, 0, 1),
    (PASS_ON, 0, 0, 3), (A2_MERGE, 3), (NEAR, 0), (NEAR, 1), (A2_FAR, 1), (A2_NEAR, 2),
    (A2_MERGE, 2), (A2_FAR, 0), (A3, 3), (A2_NEAR, 1), (A2_MERGE, 1), (A3, 2), (A3_MERGE, 3),
    (A2_NEAR, 0), (A2_MERGE, 0), (A3, 1), (A3_MERGE, 2), (UPDATE, 3), (A3, 0), (A3_MERGE, 1),
    (UPDATE, 2), (B3_FAR, 3), (A3_MERGE, 0), (UPDATE, 1), (B3_FAR, 2), (B2, 3), (UPDATE, 0),
    (B3_FAR, 1), (B2, 2), (B2_FAR, 3), (B3_FAR, 0), (B2, 1), (B2_FAR, 2), (B1_FAR, 3), (B1_NEAR, 3),
    (B2_FAR, 1), (B2, 0), (B1_MERGE, 3), (B1_FAR, 2), (B2_FAR, 0), (B1_FAR, 1), (B1_NEAR, 1),
    (B1_NEAR, 2), (B1_FAR, 0), (FINISH, 3), (B1_NEAR, 0), (B1_MERGE, 2), (B1_MERGE, 1),
    (B1_MERGE, 0), (FINISH, 1), (FINISH, 2), (FINISH, 0),
)
PACED = (A2_FAR, A3, UPDATE, B2, B2_FAR, B1_FAR, B1_MERGE)


class Piece:
    pass


class Stream:
    pass


def kernel(blocks, features, col_ids, row_ids, factor, out, *scratch):
    scratch = list(scratch)
    streams = []
    for u in range(STREAMS):
        stream = Stream()
        stream.number, stream.pieces, stream.elements_sent = u, [], 0
        for number, (start, rows) in enumerate(PIECES[u]):
            p = Piece()
            p.number, p.start, p.rows = number, start, rows
            for name, _ in PIECE_BUFFERS:
                setattr(p, name, scratch.pop(0))
            p.b1_far_up, p.b1_far_down = p.sums.at[pl.ds(1, 6)], p.sums.at[pl.ds(7, 6)]
            p.b1_up, p.b1_down = p.sums.at[pl.ds(13, 12)], p.sums.at[pl.ds(25, 12)]
            stream.pieces.append(p)
        streams.append(stream)
    (
        blk, feat, f_high, f_low, chain, a_high, a_low, part, entries, cols, col_v, col_tab, ids,
        tile, lab, tab_v, tab, x_buf, y_buf, out_buf, fac, fac_high, fac_low,
        send_sem, recv_sem, local_sem, pace_sem,
    ) = scratch

    z = lax.axis_index("gx")
    gy = lax.axis_index("gy")
    core = gy % 2
    at = {"z": z, "y": gy // 8, "x": (gy // 2) % 4}

    def neighbour(axis, step):
        to = dict(at)
        to[axis] = (at[axis] + step) % 4
        return (to["z"], to["y"] * 8 + to["x"] * 2 + core)

    sibling = (z, gy - core + (1 - core))
    counts = {"send": 0, "recv": 0, "local": 0}
    sent = []

    def take(kind, limit):
        n = counts[kind]
        counts[kind] += 1
        assert n < limit
        return n

    def arrival():
        return recv_sem.at[take("recv", N_RECV)]

    for stream in streams:
        stream.send = send_sem.at[take("send", N_SEND)]
        for p in stream.pieces:
            p.stream = stream
            p.ways = [(neighbour(axis, 1), neighbour(axis, 3)) for axis in ORDERS[p.number]]

    def remote(source, target, device, stream=None, recv=None):
        copy = pltpu.make_async_remote_copy(
            src_ref=source,
            dst_ref=target,
            send_sem=send_sem.at[take("send", N_SEND)] if stream is None else stream.send,
            recv_sem=arrival() if recv is None else recv,
            device_id=device,
            device_id_type=MESH,
        )
        copy.start()
        if stream is None:
            sent.append(copy)
        else:
            elements = 1
            for size in source.shape:
                elements *= size
            stream.elements_sent += elements
        return copy

    def wait_slots(stream, slots, sem):
        ref = entries.at[pl.ds(0, slots), stream.number]
        pltpu.make_async_copy(ref, ref, sem).wait()

    def local(source, target):
        copy = pltpu.make_async_copy(source, target, local_sem.at[take("local", N_LOCAL)])
        copy.start()
        return copy

    barrier = pltpu.get_barrier_semaphore()
    greeted = [sibling] + [neighbour(axis, step) for axis in "zyx" for step in (1, 2, 3)]
    for device in greeted:
        pl.semaphore_signal(barrier, inc=1, device_id=device, device_id_type=MESH)
    get_cols = local(col_ids, cols)
    get_ids = local(row_ids, ids)
    get_blk = {0: local(blocks.at[0], blk.at[0])}
    get_feat = [
        local(features.at[pl.ds(4 * i, 4)], feat.at[pl.ds(4 * i, 4)]) for i in range(FT // 4)
    ]
    for k in range(1, RING):
        get_blk[k] = local(blocks.at[k], blk.at[k])
    get_factor = local(factor, fac)

    get_cols.wait()
    row = lax.broadcasted_iota(I32, (BPR, BPR), 0)
    lane = lax.broadcasted_iota(I32, (BPR, BPR), 1)
    for k in range(SLOTS):
        across = jnp.broadcast_to(cols[pl.ds(k, 1), :], (BPR, BPR))
        down = jnp.sum(jnp.where(row == lane, across, 0), axis=1, keepdims=True)
        col_v[pl.ds(2 * k, 1), pl.ds(0, BPR)] = jnp.max(
            jnp.where(jnp.logical_and(down == across, row < lane), row + 1, 0), axis=0, keepdims=True
        )
        col_v[pl.ds(2 * k + 1, 1), pl.ds(0, BPR)] = jnp.max(
            jnp.where(down == lane, row + 1, 0), axis=0, keepdims=True
        )
    get_ids.wait()
    line = lax.broadcasted_iota(I32, (8, LANES), 0)
    names = jnp.full((8, LANES), -1, I32)
    for s in range(SLOTS):
        names = jnp.where(line == s, ids[s], names)
    tile[...] = names
    chain[0] = jnp.zeros((B, B), F32)
    for stream in streams:
        for p in stream.pieces:
            p.sums[0] = jnp.zeros((p.rows, LANES), F32)
            p.dense[0] = jnp.zeros((p.rows, LANES), F32)
    get_col_tab = local(col_v, col_tab)

    def convert(first):
        def body(t, carry):
            high, low = split(feat[t])
            f_high[pl.ds(pl.multiple_of(t * B, B), B), :] = high
            f_low[pl.ds(pl.multiple_of(t * B, B), B), :] = low
            return carry

        lax.fori_loop(first, first + 4, body, 0)

    def gather_sums(k):
        get_blk[k].wait()
        held = blk.at[k % RING]

        for j in range(BPR):
            chain[j + 1] = held[:, pl.ds(j * B, B)] + chain[col_tab[2 * k, j]]
        for t in range(FT):
            high, low = split(chain[col_tab[2 * k + 1, t]])
            a_high[:, pl.ds(t * B, B)] = high
            a_low[:, pl.ds(t * B, B)] = low
        if k + RING < SLOTS:
            get_blk[k + RING] = local(blocks.at[k + RING], blk.at[k % RING])

    waiting = {}
    names_recv = [arrival() for _ in ORDERS]

    def send_names(source, first):
        for j in range(3):
            for order, step in ((1, 1), (2, 3), (3, 2)):
                remote(
                    source,
                    lab.at[3 * j + order, pl.ds(first, 8)],
                    neighbour(ORDERS[j][0], step),
                    recv=names_recv[j],
                )

    def make(k):
        gather_sums(k)
        if k == 0:
            for i in range(FT // 4):
                get_feat[i].wait()
                convert(4 * i)
            pl.semaphore_wait(barrier, len(greeted))
            waiting["give"] = remote(tile, lab.at[0, pl.ds(8, 8)], sibling)
            waiting["keep"] = local(tile, lab.at[0, pl.ds(0, 8)])
            send_names(tile, 0)
        result = product(a_high[...], a_low[...], f_high[...], f_low[...])
        for half in range(2):
            for u in range(STREAMS):
                first = half * HALF + u * ROWS
                for g in range(GROUPS):
                    part[k, half, u, pl.ds(g * ROWS, ROWS), :] = result[
                        first : first + ROWS, g * LANES : (g + 1) * LANES
                    ]

    give_part = {}

    def place_of(half, chunk):
        return half * SLOTS + CHUNKS[chunk][0]

    def send_part(chunk):
        first, number = CHUNKS[chunk]
        give_part[chunk] = remote(
            part.at[pl.ds(first, number), 1 - core],
            entries.at[pl.ds(place_of(1, chunk), number)],
            sibling,
        )

    WAYS = {"up": 1, "down": 2}

    def send_list(stream, half, chunk):
        first, number = CHUNKS[chunk]
        if half == 1 and chunk not in arrived:
            arrived.add(chunk)
            give_part[chunk].wait_recv()
        stream.lists[half, chunk] = arrival()
        for p in stream.pieces:
            here = pl.ds(p.start, p.rows)
            if half == 0:
                source = part.at[pl.ds(first, number), core, stream.number, here]
            else:
                source = entries.at[pl.ds(place_of(1, chunk), number), stream.number, here]
            for name, far, device in zip(("up", "down"), (FAR_UP, FAR_DOWN), p.ways[0]):
                target = entries.at[
                    pl.ds(WAYS[name] * 12 + place_of(half, chunk), number), stream.number, here
                ]
                recv = stream.lists[half, chunk] if (half, chunk) in far else stream.list_recv
                remote(source, target, device, stream, recv)

    def send_far(stream, half, chunk):
        up = (half, chunk) in FAR_UP
        number = CHUNKS[chunk][1]
        wait_slots(stream, number, stream.lists[half, chunk])
        for p in stream.pieces:
            here = pl.ds(p.start, p.rows)
            remote(
                entries.at[
                    pl.ds(WAYS["up" if up else "down"] * 12 + place_of(half, chunk), number),
                    stream.number,
                    here,
                ],
                entries.at[pl.ds(36 + place_of(half, chunk), number), stream.number, here],
                p.ways[0][0 if up else 1],
                stream,
                stream.far_recv,
            )

    arrived = set()
    for stream in streams:
        stream.lists = {}
        stream.list_recv, stream.far_recv = arrival(), arrival()

    def make_table(j):
        held_names = lab.at[pl.ds(1 + 3 * j, 3)]
        pltpu.make_async_copy(held_names, held_names, names_recv[j]).wait()
        first, second, third = ORDERS[j]
        seen = jnp.concatenate([lab[0], lab[1 + 3 * j], lab[2 + 3 * j], lab[3 + 3 * j]], axis=0)
        row = lax.broadcasted_iota(I32, (64, LANES), 0)
        lane = lax.broadcasted_iota(I32, (64, LANES), 1)
        place_of_row = (row >> 4) * 12 + ((row >> 3) & 1) * 6 + (row & 7) + 1
        wanted = jnp.sum(jnp.where(row == lane, seen, 0), axis=0, keepdims=True)
        previous = jnp.max(
            jnp.where(jnp.logical_and(seen == wanted, row < lane), place_of_row, 0),
            axis=0,
            keepdims=True,
        )

        def step_of(order):
            return jnp.where(order == 1, 3, jnp.where(order == 2, 1, jnp.where(order == 3, 2, 0)))

        def order_of(step):
            return jnp.where(step == 0, 0, jnp.where(step == 3, 1, step + 1))

        named = (
            (at[first] << SHIFT[first])
            + (((at[second] + step_of((lane >> 3) & 3)) & 3) << SHIFT[second])
            + (((at[third] + step_of((lane >> 1) & 3)) & 3) << SHIFT[third])
            + (lane & 1)
        )
        last = jnp.max(jnp.where(seen == named, place_of_row, 0), axis=0, keepdims=True)
        place = (
            1
            + order_of((((wanted >> SHIFT[second]) & 3) - at[second]) & 3) * 8
            + order_of((((wanted >> SHIFT[third]) & 3) - at[third]) & 3) * 2
            + (wanted & 1)
        )
        place = jnp.where(((wanted >> SHIFT[first]) & 3) == at[first], place, 0)
        tab_v[j] = jnp.where(line == 0, previous, jnp.where(line == 1, last, place))

    def add_list(stream, order):
        for h in range(2):
            for slot in range(SLOTS):
                place = order * 12 + h * 6 + slot
                for p in stream.pieces:
                    here = pl.ds(p.start, p.rows)
                    if order == 0 and h == 0:
                        value = part[slot, core, stream.number, here]
                    else:
                        value = entries[place, stream.number, here]
                    p.sums[place + 1] = value + p.sums[tab[p.number, 0, order * 16 + h * 8 + slot]]

    def near_lists(stream):
        add_list(stream, 0)
        wait_slots(stream, 12, stream.list_recv)
        add_list(stream, 1)
        add_list(stream, 2)

    def pick(p, r):
        return p.sums[tab[p.number, 1, r]]

    def loop(stream, n, body):
        def step(m, carry):
            for p in stream.pieces:
                body(p, m)
            return carry

        lax.fori_loop(0, n, step, 0)

    def a2_far(stream):
        wait_slots(stream, 12, stream.far_recv)
        add_list(stream, 3)

        def body(p, m):
            p.a2_far_up[m] = pick(p, 24 + m)
            p.a2_far_down[m] = pick(p, 28 + m)

        loop(stream, 4, body)
        stream.a2_far, stream.a2_recv = arrival(), arrival()
        for p in stream.pieces:
            up, down = p.ways[1]
            remote(p.a2_far_up, p.a2_got_far_up, up, stream, stream.a2_far)
            remote(p.a2_far_down, p.a2_got_far_down, down, stream, stream.a2_far)

    def a2_near(stream):
        def body(p, m):
            p.a2_up[m + 4] = pick(p, 20 + m)
            p.a2_down[m] = pick(p, 8 + m)

        loop(stream, 4, body)
        for p in stream.pieces:
            up, down = p.ways[1]
            remote(p.a2_up.at[pl.ds(4, 4)], p.a2_got.at[pl.ds(4, 4)], up, stream, stream.a2_recv)
            remote(p.a2_down.at[pl.ds(0, 4)], p.a2_got.at[pl.ds(8, 4)], down, stream, stream.a2_recv)

    def a2_merge(stream):
        wait_slots(stream, 8, stream.a2_far)

        def body(p, m):
            p.a2_up[m] = p.a2_got_far_up[m] + pick(p, 16 + m)
            p.a2_down[m + 4] = p.a2_got_far_down[m] + pick(p, 12 + m)

        loop(stream, 4, body)
        for p in stream.pieces:
            up, down = p.ways[1]
            remote(p.a2_up.at[pl.ds(0, 4)], p.a2_got.at[pl.ds(0, 4)], up, stream, stream.a2_recv)
            remote(p.a2_down.at[pl.ds(4, 4)], p.a2_got.at[pl.ds(12, 4)], down, stream, stream.a2_recv)

    def a3_start(stream):
        wait_slots(stream, 16, stream.a2_recv)

        def body(p, m):
            p.quarter[m] = pick(p, m) + (p.a2_got[m] + p.a2_got[8 + m])

        loop(stream, 8, body)
        stream.a3_far, stream.a3_recv = arrival(), arrival()
        for p in stream.pieces:
            up, down = p.ways[2]
            remote(p.quarter.at[6], p.a3_got_far.at[0], up, stream, stream.a3_far)
            remote(p.quarter.at[7], p.a3_got_far.at[1], down, stream, stream.a3_far)
        for p in stream.pieces:
            up, down = p.ways[2]
            remote(p.quarter.at[5], p.a3_got.at[1], up, stream, stream.a3_recv)
            remote(p.quarter.at[2], p.a3_got.at[2], down, stream, stream.a3_recv)

    def a3_merge(stream):
        wait_slots(stream, 2, stream.a3_far)
        for p in stream.pieces:
            p.a3_up[0] = p.quarter[4] + p.a3_got_far[0]
            p.a3_down[0] = p.quarter[3] + p.a3_got_far[1]
        for p in stream.pieces:
            up, down = p.ways[2]
            remote(p.a3_up.at[0], p.a3_got.at[0], up, stream, stream.a3_recv)
            remote(p.a3_down.at[0], p.a3_got.at[3], down, stream, stream.a3_recv)

    last = []

    def update(stream):
        u = stream.number
        wait_slots(stream, 4, stream.a3_recv)
        for p in stream.pieces:
            for b in range(2):
                x_buf[u, b, pl.ds(p.start, p.rows), :] = jnp.tanh(
                    p.quarter[b] + (p.a3_got[b] + p.a3_got[2 + b])
                )
        x = jnp.concatenate(
            [
                jnp.concatenate(
                    [x_buf[u, b, pl.ds(g * ROWS, ROWS), :] for g in range(GROUPS)], axis=1
                )
                for b in range(2)
            ],
            axis=0,
        )
        x_high, x_low = split(x)
        y = product(x_high, x_low, fac_high[...], fac_low[...])
        for b in range(2):
            rows_y = y[b * ROWS : (b + 1) * ROWS]
            flat = jnp.concatenate(
                [rows_y[:, g * LANES : (g + 1) * LANES] for g in range(GROUPS)], axis=0
            )
            for p in stream.pieces:
                p.dense[1 + b] = flat[p.start : p.start + p.rows]
        stream.b3_far, stream.b3_recv = arrival(), arrival()
        for p in stream.pieces:
            d, (up, down) = p.dense, p.ways[2]
            remote(d.at[1], d.at[3], up, stream, stream.b3_far)
            remote(d.at[2], d.at[6], down, stream, stream.b3_far)
        for p in stream.pieces:
            d, (up, down) = p.dense, p.ways[2]
            remote(d.at[2], d.at[4], up, stream, stream.b3_recv)
            remote(d.at[1], d.at[5], down, stream, stream.b3_recv)
        here = pl.ds(pl.multiple_of(core * HALF + u * ROWS, ROWS), ROWS)
        out[0, here, :] = jnp.where(core == 0, y[:ROWS], y[ROWS:])
        y_buf[u] = jnp.where(core == 0, y[ROWS:], y[:ROWS])
        last.append(remote(y_buf.at[u], out.at[0, here, :], sibling))

    def b3_far(stream):
        wait_slots(stream, 2, stream.b3_far)
        for p in stream.pieces:
            d, (up, down) = p.dense, p.ways[2]
            remote(d.at[3], d.at[7], up, stream, stream.b3_recv)
            remote(d.at[6], d.at[8], down, stream, stream.b3_recv)

    def b2_start(stream):
        wait_slots(stream, 4, stream.b3_recv)
        stream.b2_far, stream.b2_recv = arrival(), arrival()
        for p in stream.pieces:
            d, (up, down) = p.dense, p.ways[1]
            remote(d.at[pl.ds(1, 4)], d.at[pl.ds(9, 4)], up, stream, stream.b2_far)
            remote(d.at[pl.ds(5, 4)], d.at[pl.ds(21, 4)], down, stream, stream.b2_far)
        for p in stream.pieces:
            d, (up, down) = p.dense, p.ways[1]
            remote(d.at[pl.ds(5, 4)], d.at[pl.ds(13, 4)], up, stream, stream.b2_recv)
            remote(d.at[pl.ds(1, 4)], d.at[pl.ds(17, 4)], down, stream, stream.b2_recv)

    def b2_far(stream):
        wait_slots(stream, 8, stream.b2_far)
        for p in stream.pieces:
            d, (up, down) = p.dense, p.ways[1]
            remote(d.at[pl.ds(9, 4)], d.at[pl.ds(25, 4)], up, stream, stream.b2_recv)
            remote(d.at[pl.ds(21, 4)], d.at[pl.ds(29, 4)], down, stream, stream.b2_recv)

    def answer(p, i):
        return p.dense[tab[p.number, 2, i]]

    def b1_far(stream):
        wait_slots(stream, 16, stream.b2_recv)

        def body(p, h):
            for s in range(3):
                p.b1_far_up[h * 3 + s] = answer(p, 48 + h * 8 + s)
                p.b1_far_down[h * 3 + s] = answer(p, 51 + h * 8 + s)

        loop(stream, 2, body)
        stream.b1_far, stream.b1_recv = arrival(), arrival()
        for p in stream.pieces:
            up, down = p.ways[0]
            remote(p.b1_far_up, p.b1_got_far_up, up, stream, stream.b1_far)
            remote(p.b1_far_down, p.b1_got_far_down, down, stream, stream.b1_far)

    def b1_near(stream):
        def body(p, h):
            for s in range(3):
                p.b1_up[6 + h * 3 + s] = answer(p, 35 + h * 8 + s)
                p.b1_down[h * 3 + s] = answer(p, 16 + h * 8 + s)

        loop(stream, 2, body)
        for p in stream.pieces:
            up, down = p.ways[0]
            remote(p.b1_up.at[pl.ds(6, 6)], p.b1_got.at[pl.ds(6, 6)], up, stream, stream.b1_recv)
            remote(p.b1_down.at[pl.ds(0, 6)], p.b1_got.at[pl.ds(12, 6)], down, stream, stream.b1_recv)

    def b1_merge(stream):
        wait_slots(stream, 12, stream.b1_far)

        def body(p, h):
            for s in range(3):
                p.b1_up[h * 3 + s] = p.b1_got_far_up[h * 3 + s] + answer(p, 32 + h * 8 + s)
                p.b1_down[6 + h * 3 + s] = p.b1_got_far_down[h * 3 + s] + answer(p, 19 + h * 8 + s)

        loop(stream, 2, body)
        for p in stream.pieces:
            up, down = p.ways[0]
            remote(p.b1_up.at[pl.ds(0, 6)], p.b1_got.at[pl.ds(0, 6)], up, stream, stream.b1_recv)
            remote(p.b1_down.at[pl.ds(6, 6)], p.b1_got.at[pl.ds(18, 6)], down, stream, stream.b1_recv)

    def finish(stream):
        u = stream.number
        first = core * HALF + u * ROWS
        wait_slots(stream, 24, stream.b1_recv)

        def body(p, n):
            t, s = n // 3, n % 3
            for h in (1, 0):
                q = t * 6 + h * 3 + s
                value = answer(p, h * 8 + n) + (p.b1_got[q] + p.b1_got[12 + q])
                done = 0
                while done < p.rows:
                    g, r = divmod(p.start + done, ROWS)
                    size = min(ROWS - r, p.rows - done)
                    across = pl.ds(g * LANES, LANES)
                    if h == 0:
                        rows = pl.ds(pl.multiple_of(first + r, 8), size)
                        out[1 + n, rows, across] = value[done : done + size]
                    else:
                        out_buf[u, n, pl.ds(r, size), across] = value[done : done + size]
                    done += size

        loop(stream, SLOTS, body)
        here = pl.ds(pl.multiple_of(first, ROWS), ROWS)
        last.append(remote(out_buf.at[u], out.at[pl.ds(1, SLOTS), here, :], sibling))

    get_col_tab.wait()

    def product_block(k):
        make(k)
        if k == 0:
            waiting["give"].wait_recv()
            send_names(lab.at[0, pl.ds(8, 8)], 8)

    def tables():
        waiting["keep"].wait()
        for j in range(3):
            make_table(j)
        get_factor.wait()
        high, low = split(fac[...])
        fac_high[...] = high
        fac_low[...] = low
        local(tab_v, tab).wait()

    blocks_of = {
        MAKE: product_block, GIVE: send_part, SEND: send_list, PASS_ON: send_far, TABLES: tables,
        NEAR: near_lists, A2_FAR: a2_far, A2_NEAR: a2_near, A2_MERGE: a2_merge, A3: a3_start,
        A3_MERGE: a3_merge, UPDATE: update, B3_FAR: b3_far, B2: b2_start, B2_FAR: b2_far,
        B1_FAR: b1_far, B1_NEAR: b1_near, B1_MERGE: b1_merge, FINISH: finish,
    }
    paced = 0
    for kind, *numbers in ORDER:
        if kind in PACED:
            pl.semaphore_signal(pace_sem, inc=1, device_id=sibling, device_id_type=MESH)
            if paced:
                pl.semaphore_wait(pace_sem, 1)
            paced += 1
        if kind in (MAKE, GIVE, TABLES):
            blocks_of[kind](*numbers)
        else:
            blocks_of[kind](streams[numbers[0]], *numbers[1:])
    pl.semaphore_wait(pace_sem, 1)
    for copy in last:
        copy.wait_recv()
    for copy in sent:
        copy.wait_send()
    for stream in streams:
        assert stream.elements_sent == STREAM_SLOTS * TILE_ROWS * LANES
        ref = blocks.at[:, pl.ds(0, 88), pl.ds(0, 32 * TILE_ROWS)]
        pltpu.make_async_copy(ref, ref, stream.send).wait()


def output_kernel(held, owned, returned, sems):
    copies = (
        pltpu.make_async_copy(held.at[0], owned, sems.at[0]),
        pltpu.make_async_copy(held.at[pl.ds(1, SLOTS)], returned, sems.at[1]),
    )
    for copy in copies:
        copy.start()
    for copy in copies:
        copy.wait()


def local_step(blocks, features, col_ids, row_ids, factor):
    scratch = []
    for u in range(STREAMS):
        for _, rows in PIECES[u]:
            for _, depth in PIECE_BUFFERS:
                scratch.append(pltpu.VMEM((depth, rows, LANES), F32))
    scratch += [
        pltpu.VMEM((RING, B, BPR * B), F32),
        pltpu.VMEM((FT, B, FEAT), F32),
        pltpu.VMEM((FT * B, FEAT), BF16),
        pltpu.VMEM((FT * B, FEAT), BF16),
        pltpu.VMEM((BPR + 1, B, B), F32),
        pltpu.VMEM((B, FT * B), BF16),
        pltpu.VMEM((B, FT * B), BF16),
        pltpu.VMEM((SLOTS, 2, STREAMS, TILE_ROWS, LANES), F32),
        pltpu.VMEM((48, STREAMS, TILE_ROWS, LANES), F32),
        pltpu.VMEM((SLOTS, BPR), I32),
        pltpu.VMEM((16, LANES), I32),
        pltpu.SMEM((16, LANES), I32),
        pltpu.SMEM((SLOTS,), I32),
        pltpu.VMEM((8, LANES), I32),
        pltpu.VMEM((10, 16, LANES), I32),
        pltpu.VMEM((3, 8, LANES), I32),
        pltpu.SMEM((3, 8, LANES), I32),
        pltpu.VMEM((STREAMS, 2, TILE_ROWS, LANES), F32),
        pltpu.VMEM((STREAMS, ROWS, FEAT), F32),
        pltpu.VMEM((STREAMS, SLOTS, ROWS, FEAT), F32),
        pltpu.VMEM((FEAT, FEAT), F32),
        pltpu.VMEM((FEAT, FEAT), BF16),
        pltpu.VMEM((FEAT, FEAT), BF16),
        pltpu.SemaphoreType.DMA((N_SEND,)),
        pltpu.SemaphoreType.DMA((N_RECV,)),
        pltpu.SemaphoreType.DMA((N_LOCAL,)),
        pltpu.SemaphoreType.REGULAR,
    ]
    hbm = pl.BlockSpec(memory_space=pl.ANY)
    held = pl.pallas_call(
        kernel,
        in_specs=[hbm] * 5,
        out_specs=pl.BlockSpec(memory_space=pltpu.VMEM),
        out_shape=pltpu.VMEM((1 + SLOTS, B, FEAT), F32),
        scratch_shapes=scratch,
        compiler_params=pltpu.CompilerParams(
            collective_id=0, has_side_effects=True, vmem_limit_bytes=VMEM_LIMIT
        ),
    )(blocks, features, col_ids, row_ids, factor)
    owned, returned = pl.pallas_call(
        output_kernel,
        in_specs=[pl.BlockSpec(memory_space=pltpu.VMEM)],
        out_specs=[hbm] * 2,
        out_shape=[
            jax.ShapeDtypeStruct((B, FEAT), F32),
            jax.ShapeDtypeStruct((SLOTS, B, FEAT), F32),
        ],
        scratch_shapes=[pltpu.SemaphoreType.DMA((2,))],
        compiler_params=pltpu.CompilerParams(vmem_limit_bytes=1 << 20),
    )(held)
    return owned, returned.reshape(SLOTS * B, FEAT)


def solution(mesh):
    return jax.shard_map(
        local_step,
        mesh=mesh,
        in_specs=(
            P(("gx", "gy"), None, None),
            P(("gx", "gy"), None, None),
            P(("gx", "gy"), None),
            P(("gx", "gy")),
            P(),
        ),
        out_specs=(P(("gx", "gy"), None), P(("gx", "gy"), None)),
        check_vma=False,
    )
```

```python
import functools

import jax
import jax.numpy as jnp
from jax import lax
from jax.experimental import pallas as pl
from jax.experimental.pallas import tpu as pltpu
from jax.sharding import PartitionSpec as P

MESH = pl.DeviceIdType.MESH
F32 = jnp.float32
BF16 = jnp.bfloat16
I32 = jnp.int32

B = 128
FEAT = 512
SLOTS = 6
BPR = 32
FT = 16
HALF = B // 2
STREAMS = 4
ROWS = HALF // STREAMS
LANES = 128
GROUPS = FEAT // LANES
TILE_ROWS = ROWS * GROUPS
SHIFT = {"z": 5, "y": 3, "x": 1}
ORDERS = ("zyx", "yxz", "xzy")
SECOND_ORDERS = ("zyx", "xzy", "yxz")
PIECES = (
    ((0, 24), (24, 24), (48, 16)),
    ((0, 24), (24, 16), (40, 24)),
    ((0, 16), (16, 24), (40, 24)),
    ((0, 24), (24, 24), (48, 16)),
)
CHUNKS = ((0, 1), (1, 1), (2, 2), (4, 2))
FAR_UP = ((0, 0), (1, 0), (0, 1), (1, 1), (0, 3))
FAR_DOWN = ((0, 2), (1, 2), (1, 3))


def split(value):
    high = value.astype(BF16)
    return high, (value - high.astype(F32)).astype(BF16)


def product(left_high, left_low, right_high, right_low):
    dot = functools.partial(jnp.dot, preferred_element_type=F32)
    return dot(left_high, right_high) + (dot(left_high, right_low) + dot(left_low, right_high))


PIECE_BUFFERS = (
    ("sums", 49),
    ("a2_far_up", 4),
    ("a2_far_down", 4),
    ("a2_got_far_up", 4),
    ("a2_got_far_down", 4),
    ("a2_up", 8),
    ("a2_down", 8),
    ("a2_got", 16),
    ("quarter", 8),
    ("a3_got_far", 2),
    ("a3_up", 1),
    ("a3_down", 1),
    ("a3_got", 4),
    ("dense", 33),
    ("b1_got_far_up", 6),
    ("b1_got_far_down", 6),
    ("b1_got", 24),
)
STREAM_SLOTS = 36 + 24 + 6 + 6 + 24 + 36
N_SEND = 35
N_RECV = 96
N_LOCAL = 16
RING = 4
VMEM_LIMIT = 58 << 20

(
    MAKE, GIVE, SEND, PASS_ON, TABLES, NEAR, A2_FAR, A2_NEAR, A2_MERGE, A3,
    A3_MERGE, UPDATE, B3_FAR, B2, B2_FAR, B1_FAR, B1_NEAR, B1_MERGE, FINISH,
) = range(19)
ORDER = (
    (MAKE, 0), (GIVE, 0), (SEND, 0, 0, 0), (SEND, 1, 0, 0), (MAKE, 1), (GIVE, 1), (SEND, 2, 0, 0),
    (SEND, 2, 1, 0), (SEND, 2, 0, 1), (SEND, 3, 0, 0), (SEND, 0, 1, 0), (SEND, 1, 1, 0),
    (SEND, 3, 0, 1), (MAKE, 2), (SEND, 1, 0, 1), (SEND, 3, 1, 1), (SEND, 0, 1, 1), (SEND, 3, 1, 0),
    (SEND, 0, 0, 1), (SEND, 1, 1, 1), (MAKE, 3), (GIVE, 2), (SEND, 2, 0, 2), (SEND, 1, 0, 2),
    (SEND, 0, 0, 2), (SEND, 2, 1, 1), (SEND, 3, 0, 2), (MAKE, 4), (SEND, 3, 1, 2), (SEND, 2, 1, 2),
    (MAKE, 5), (GIVE, 3), (SEND, 3, 0, 3), (PASS_ON, 3, 1, 1), (PASS_ON, 3, 0, 0), (SEND, 2, 0, 3),
    (SEND, 3, 1, 3), (PASS_ON, 1, 0, 2), (PASS_ON, 2, 1, 0), (SEND, 1, 1, 2), (PASS_ON, 3, 0, 1),
    (SEND, 1, 1, 3), (SEND, 2, 1, 3), (SEND, 0, 1, 3), (PASS_ON, 3, 1, 0), (TABLES,),
    (PASS_ON, 2, 0, 0), (PASS_ON, 3, 0, 2), (PASS_ON, 3, 1, 2), (PASS_ON, 3, 0, 3),
    (PASS_ON, 1, 1, 1), (PASS_ON, 1, 0, 1), (PASS_ON, 3, 1, 3), (PASS_ON, 1, 0, 0),
    (PASS_ON, 2, 0, 2), (SEND, 1, 0, 3), (PASS_ON, 2, 1, 1), (PASS_ON, 2, 1, 2), (PASS_ON, 0, 0, 2),
    (NEAR, 3), (PASS_ON, 0, 1, 0), (PASS_ON, 2, 0, 3), (PASS_ON, 2, 0, 1), (PASS_ON, 2, 1, 3),
    (PASS_ON, 1, 1, 2), (SEND, 0, 0, 3), (PASS_ON, 1, 1, 0), (SEND, 0, 1, 2), (A2_FAR, 3),
    (PASS_ON, 1, 1, 3), (PASS_ON, 1, 0, 3), (PASS_ON, 0, 1, 3), (PASS_ON, 0, 0, 0), (A2_NEAR, 3),
    (NEAR, 2), (PASS_ON, 0, 1, 1), (A2_FAR, 2), (PASS_ON, 0, 1, 2), (PASS_ON, 0, 0, 1),
    (PASS_ON, 0, 0, 3), (A2_MERGE, 3), (NEAR, 0), (NEAR, 1), (A2_FAR, 1), (A2_NEAR, 2),
    (A2_MERGE, 2), (A2_FAR, 0), (A3, 3), (A2_NEAR, 1), (A2_MERGE, 1), (A3, 2), (A3_MERGE, 3),
    (A2_NEAR, 0), (A2_MERGE, 0), (A3, 1), (A3_MERGE, 2), (UPDATE, 3), (A3, 0), (A3_MERGE, 1),
    (UPDATE, 2), (B3_FAR, 3), (A3_MERGE, 0), (UPDATE, 1), (B3_FAR, 2), (B2, 3), (UPDATE, 0),
    (B3_FAR, 1), (B2, 2), (B2_FAR, 3), (B3_FAR, 0), (B2, 1), (B2_FAR, 2), (B1_FAR, 3), (B1_NEAR, 3),
    (B2_FAR, 1), (B2, 0), (B1_MERGE, 3), (B1_FAR, 2), (B2_FAR, 0), (B1_FAR, 1), (B1_NEAR, 1),
    (B1_NEAR, 2), (B1_FAR, 0), (FINISH, 3), (B1_NEAR, 0), (B1_MERGE, 2), (B1_MERGE, 1),
    (B1_MERGE, 0), (FINISH, 1), (FINISH, 2), (FINISH, 0),
)
PACED = (A2_FAR, A3, UPDATE, B2, B2_FAR, B1_FAR, B1_MERGE)


class Piece:
    pass


class Stream:
    pass


def kernel(blocks, features, col_ids, row_ids, factor, out, *scratch):
    scratch = list(scratch)
    streams = []
    for u in range(STREAMS):
        stream = Stream()
        stream.number, stream.pieces, stream.elements_sent = u, [], 0
        for number, (start, rows) in enumerate(PIECES[u]):
            p = Piece()
            p.number, p.start, p.rows = number, start, rows
            for name, _ in PIECE_BUFFERS:
                setattr(p, name, scratch.pop(0))
            p.b1_far_up, p.b1_far_down = p.sums.at[pl.ds(1, 6)], p.sums.at[pl.ds(7, 6)]
            p.b1_up, p.b1_down = p.sums.at[pl.ds(13, 12)], p.sums.at[pl.ds(25, 12)]
            stream.pieces.append(p)
        streams.append(stream)
    (
        blk, feat, f_high, f_low, chain, a_high, a_low, part, entries, cols, col_v, col_tab, ids,
        tile, lab, tab_v, tab, x_buf, y_buf, out_buf, fac, fac_high, fac_low,
        send_sem, recv_sem, local_sem, pace_sem,
    ) = scratch

    z = lax.axis_index("gx")
    gy = lax.axis_index("gy")
    core = gy % 2
    at = {"z": z, "y": gy // 8, "x": (gy // 2) % 4}

    def neighbour(axis, step):
        to = dict(at)
        to[axis] = (at[axis] + step) % 4
        return (to["z"], to["y"] * 8 + to["x"] * 2 + core)

    def blend(first, second):
        return first if first is second else first + core * (second - first)

    def ring(number, phase, step):
        here = neighbour(ORDERS[number][phase], step)
        there = neighbour(SECOND_ORDERS[number][phase], step)
        if ORDERS[number] == SECOND_ORDERS[number]:
            return here
        return tuple(blend(a, b) for a, b in zip(here, there))

    sibling = (z, gy - core + (1 - core))
    counts = {"send": 0, "recv": 0, "local": 0}
    sent = []

    def take(kind, limit):
        n = counts[kind]
        counts[kind] += 1
        assert n < limit
        return n

    def arrival():
        return recv_sem.at[take("recv", N_RECV)]

    for stream in streams:
        stream.send = send_sem.at[take("send", N_SEND)]
        for p in stream.pieces:
            p.stream = stream
            p.ways = [(ring(p.number, i, 1), ring(p.number, i, 3)) for i in range(3)]

    def remote(source, target, device, stream=None, recv=None):
        copy = pltpu.make_async_remote_copy(
            src_ref=source,
            dst_ref=target,
            send_sem=send_sem.at[take("send", N_SEND)] if stream is None else stream.send,
            recv_sem=arrival() if recv is None else recv,
            device_id=device,
            device_id_type=MESH,
        )
        copy.start()
        if stream is None:
            sent.append(copy)
        else:
            elements = 1
            for size in source.shape:
                elements *= size
            stream.elements_sent += elements
        return copy

    def wait_slots(stream, slots, sem):
        ref = entries.at[pl.ds(0, slots), stream.number]
        pltpu.make_async_copy(ref, ref, sem).wait()

    def local(source, target):
        copy = pltpu.make_async_copy(source, target, local_sem.at[take("local", N_LOCAL)])
        copy.start()
        return copy

    barrier = pltpu.get_barrier_semaphore()
    greeted = [sibling] + [neighbour(axis, step) for axis in "zyx" for step in (1, 2, 3)]
    for device in greeted:
        pl.semaphore_signal(barrier, inc=1, device_id=device, device_id_type=MESH)
    get_cols = local(col_ids, cols)
    get_ids = local(row_ids, ids)
    get_blk = {0: local(blocks.at[0], blk.at[0])}
    get_feat = [
        local(features.at[pl.ds(4 * i, 4)], feat.at[pl.ds(4 * i, 4)]) for i in range(FT // 4)
    ]
    for k in range(1, RING):
        get_blk[k] = local(blocks.at[k], blk.at[k])
    get_factor = local(factor, fac)

    get_cols.wait()
    row = lax.broadcasted_iota(I32, (BPR, BPR), 0)
    lane = lax.broadcasted_iota(I32, (BPR, BPR), 1)
    for k in range(SLOTS):
        across = jnp.broadcast_to(cols[pl.ds(k, 1), :], (BPR, BPR))
        down = jnp.sum(jnp.where(row == lane, across, 0), axis=1, keepdims=True)
        col_v[pl.ds(2 * k, 1), pl.ds(0, BPR)] = jnp.max(
            jnp.where(jnp.logical_and(down == across, row < lane), row + 1, 0), axis=0, keepdims=True
        )
        col_v[pl.ds(2 * k + 1, 1), pl.ds(0, BPR)] = jnp.max(
            jnp.where(down == lane, row + 1, 0), axis=0, keepdims=True
        )
    get_ids.wait()
    line = lax.broadcasted_iota(I32, (8, LANES), 0)
    names = jnp.full((8, LANES), -1, I32)
    for s in range(SLOTS):
        names = jnp.where(line == s, ids[s], names)
    tile[...] = names
    chain[0] = jnp.zeros((B, B), F32)
    for stream in streams:
        for p in stream.pieces:
            p.sums[0] = jnp.zeros((p.rows, LANES), F32)
            p.dense[0] = jnp.zeros((p.rows, LANES), F32)
    get_col_tab = local(col_v, col_tab)

    def convert(first):
        def body(t, carry):
            high, low = split(feat[t])
            f_high[pl.ds(pl.multiple_of(t * B, B), B), :] = high
            f_low[pl.ds(pl.multiple_of(t * B, B), B), :] = low
            return carry

        lax.fori_loop(first, first + 4, body, 0)

    def gather_sums(k):
        get_blk[k].wait()
        held = blk.at[k % RING]

        for j in range(BPR):
            chain[j + 1] = held[:, pl.ds(j * B, B)] + chain[col_tab[2 * k, j]]
        for t in range(FT):
            high, low = split(chain[col_tab[2 * k + 1, t]])
            a_high[:, pl.ds(t * B, B)] = high
            a_low[:, pl.ds(t * B, B)] = low
        if k + RING < SLOTS:
            get_blk[k + RING] = local(blocks.at[k + RING], blk.at[k % RING])

    waiting = {}
    names_recv = [arrival() for _ in ORDERS]

    def send_names(source, first):
        for j in range(3):
            for order, step in ((1, 1), (2, 3), (3, 2)):
                remote(
                    source,
                    lab.at[3 * j + order, pl.ds(first, 8)],
                    ring(j, 0, step),
                    recv=names_recv[j],
                )

    def make(k):
        gather_sums(k)
        if k == 0:
            for i in range(FT // 4):
                get_feat[i].wait()
                convert(4 * i)
            pl.semaphore_wait(barrier, len(greeted))
            waiting["give"] = remote(tile, lab.at[0, pl.ds(8, 8)], sibling)
            waiting["keep"] = local(tile, lab.at[0, pl.ds(0, 8)])
            send_names(tile, 0)
        result = product(a_high[...], a_low[...], f_high[...], f_low[...])
        for half in range(2):
            for u in range(STREAMS):
                first = half * HALF + u * ROWS
                for g in range(GROUPS):
                    part[k, half, u, pl.ds(g * ROWS, ROWS), :] = result[
                        first : first + ROWS, g * LANES : (g + 1) * LANES
                    ]

    give_part = {}

    def place_of(half, chunk):
        return half * SLOTS + CHUNKS[chunk][0]

    def send_part(chunk):
        first, number = CHUNKS[chunk]
        give_part[chunk] = remote(
            part.at[pl.ds(first, number), 1 - core],
            entries.at[pl.ds(place_of(1, chunk), number)],
            sibling,
        )

    WAYS = {"up": 1, "down": 2}

    def send_list(stream, half, chunk):
        first, number = CHUNKS[chunk]
        if half == 1 and chunk not in arrived:
            arrived.add(chunk)
            give_part[chunk].wait_recv()
        stream.lists[half, chunk] = arrival()
        for p in stream.pieces:
            here = pl.ds(p.start, p.rows)
            if half == 0:
                source = part.at[pl.ds(first, number), core, stream.number, here]
            else:
                source = entries.at[pl.ds(place_of(1, chunk), number), stream.number, here]
            for name, far, device in zip(("up", "down"), (FAR_UP, FAR_DOWN), p.ways[0]):
                target = entries.at[
                    pl.ds(WAYS[name] * 12 + place_of(half, chunk), number), stream.number, here
                ]
                recv = stream.lists[half, chunk] if (half, chunk) in far else stream.list_recv
                remote(source, target, device, stream, recv)

    def send_far(stream, half, chunk):
        up = (half, chunk) in FAR_UP
        number = CHUNKS[chunk][1]
        wait_slots(stream, number, stream.lists[half, chunk])
        for p in stream.pieces:
            here = pl.ds(p.start, p.rows)
            remote(
                entries.at[
                    pl.ds(WAYS["up" if up else "down"] * 12 + place_of(half, chunk), number),
                    stream.number,
                    here,
                ],
                entries.at[pl.ds(36 + place_of(half, chunk), number), stream.number, here],
                p.ways[0][0 if up else 1],
                stream,
                stream.far_recv,
            )

    arrived = set()
    for stream in streams:
        stream.lists = {}
        stream.list_recv, stream.far_recv = arrival(), arrival()

    def make_table(j):
        held_names = lab.at[pl.ds(1 + 3 * j, 3)]
        pltpu.make_async_copy(held_names, held_names, names_recv[j]).wait()
        own = [blend(at[a], at[b]) for a, b in zip(ORDERS[j], SECOND_ORDERS[j])]
        stride = [
            blend(1 << SHIFT[a], 1 << SHIFT[b]) for a, b in zip(ORDERS[j], SECOND_ORDERS[j])
        ]
        seen = jnp.concatenate([lab[0], lab[1 + 3 * j], lab[2 + 3 * j], lab[3 + 3 * j]], axis=0)
        row = lax.broadcasted_iota(I32, (64, LANES), 0)
        lane = lax.broadcasted_iota(I32, (64, LANES), 1)
        place_of_row = (row >> 4) * 12 + ((row >> 3) & 1) * 6 + (row & 7) + 1
        wanted = jnp.sum(jnp.where(row == lane, seen, 0), axis=0, keepdims=True)
        previous = jnp.max(
            jnp.where(jnp.logical_and(seen == wanted, row < lane), place_of_row, 0),
            axis=0,
            keepdims=True,
        )

        def step_of(order):
            return jnp.where(order == 1, 3, jnp.where(order == 2, 1, jnp.where(order == 3, 2, 0)))

        def order_of(step):
            return jnp.where(step == 0, 0, jnp.where(step == 3, 1, step + 1))

        named = (
            own[0] * stride[0]
            + ((own[1] + step_of((lane >> 3) & 3)) & 3) * stride[1]
            + ((own[2] + step_of((lane >> 1) & 3)) & 3) * stride[2]
            + (lane & 1)
        )
        last = jnp.max(jnp.where(seen == named, place_of_row, 0), axis=0, keepdims=True)
        at_axis = [
            (wanted >> SHIFT[a]) & 3
            if ORDERS[j] == SECOND_ORDERS[j]
            else blend((wanted >> SHIFT[a]) & 3, (wanted >> SHIFT[b]) & 3)
            for a, b in zip(ORDERS[j], SECOND_ORDERS[j])
        ]
        place = (
            1
            + order_of((at_axis[1] - own[1]) & 3) * 8
            + order_of((at_axis[2] - own[2]) & 3) * 2
            + (wanted & 1)
        )
        place = jnp.where(at_axis[0] == own[0], place, 0)
        tab_v[j] = jnp.where(line == 0, previous, jnp.where(line == 1, last, place))

    def add_list(stream, order):
        for h in range(2):
            for slot in range(SLOTS):
                place = order * 12 + h * 6 + slot
                for p in stream.pieces:
                    here = pl.ds(p.start, p.rows)
                    if order == 0 and h == 0:
                        value = part[slot, core, stream.number, here]
                    else:
                        value = entries[place, stream.number, here]
                    p.sums[place + 1] = value + p.sums[tab[p.number, 0, order * 16 + h * 8 + slot]]

    def near_lists(stream):
        add_list(stream, 0)
        wait_slots(stream, 12, stream.list_recv)
        add_list(stream, 1)
        add_list(stream, 2)

    def pick(p, r):
        return p.sums[tab[p.number, 1, r]]

    def loop(stream, n, body):
        def step(m, carry):
            for p in stream.pieces:
                body(p, m)
            return carry

        lax.fori_loop(0, n, step, 0)

    def a2_far(stream):
        wait_slots(stream, 12, stream.far_recv)
        add_list(stream, 3)

        def body(p, m):
            p.a2_far_up[m] = pick(p, 24 + m)
            p.a2_far_down[m] = pick(p, 28 + m)

        loop(stream, 4, body)
        stream.a2_far, stream.a2_recv = arrival(), arrival()
        for p in stream.pieces:
            up, down = p.ways[1]
            remote(p.a2_far_up, p.a2_got_far_up, up, stream, stream.a2_far)
            remote(p.a2_far_down, p.a2_got_far_down, down, stream, stream.a2_far)

    def a2_near(stream):
        def body(p, m):
            p.a2_up[m + 4] = pick(p, 20 + m)
            p.a2_down[m] = pick(p, 8 + m)

        loop(stream, 4, body)
        for p in stream.pieces:
            up, down = p.ways[1]
            remote(p.a2_up.at[pl.ds(4, 4)], p.a2_got.at[pl.ds(4, 4)], up, stream, stream.a2_recv)
            remote(p.a2_down.at[pl.ds(0, 4)], p.a2_got.at[pl.ds(8, 4)], down, stream, stream.a2_recv)

    def a2_merge(stream):
        wait_slots(stream, 8, stream.a2_far)

        def body(p, m):
            p.a2_up[m] = p.a2_got_far_up[m] + pick(p, 16 + m)
            p.a2_down[m + 4] = p.a2_got_far_down[m] + pick(p, 12 + m)

        loop(stream, 4, body)
        for p in stream.pieces:
            up, down = p.ways[1]
            remote(p.a2_up.at[pl.ds(0, 4)], p.a2_got.at[pl.ds(0, 4)], up, stream, stream.a2_recv)
            remote(p.a2_down.at[pl.ds(4, 4)], p.a2_got.at[pl.ds(12, 4)], down, stream, stream.a2_recv)

    def a3_start(stream):
        wait_slots(stream, 16, stream.a2_recv)

        def body(p, m):
            p.quarter[m] = pick(p, m) + (p.a2_got[m] + p.a2_got[8 + m])

        loop(stream, 8, body)
        stream.a3_far, stream.a3_recv = arrival(), arrival()
        for p in stream.pieces:
            up, down = p.ways[2]
            remote(p.quarter.at[6], p.a3_got_far.at[0], up, stream, stream.a3_far)
            remote(p.quarter.at[7], p.a3_got_far.at[1], down, stream, stream.a3_far)
        for p in stream.pieces:
            up, down = p.ways[2]
            remote(p.quarter.at[5], p.a3_got.at[1], up, stream, stream.a3_recv)
            remote(p.quarter.at[2], p.a3_got.at[2], down, stream, stream.a3_recv)

    def a3_merge(stream):
        wait_slots(stream, 2, stream.a3_far)
        for p in stream.pieces:
            p.a3_up[0] = p.quarter[4] + p.a3_got_far[0]
            p.a3_down[0] = p.quarter[3] + p.a3_got_far[1]
        for p in stream.pieces:
            up, down = p.ways[2]
            remote(p.a3_up.at[0], p.a3_got.at[0], up, stream, stream.a3_recv)
            remote(p.a3_down.at[0], p.a3_got.at[3], down, stream, stream.a3_recv)

    last = []

    def update(stream):
        u = stream.number
        wait_slots(stream, 4, stream.a3_recv)
        for p in stream.pieces:
            for b in range(2):
                x_buf[u, b, pl.ds(p.start, p.rows), :] = jnp.tanh(
                    p.quarter[b] + (p.a3_got[b] + p.a3_got[2 + b])
                )
        x = jnp.concatenate(
            [
                jnp.concatenate(
                    [x_buf[u, b, pl.ds(g * ROWS, ROWS), :] for g in range(GROUPS)], axis=1
                )
                for b in range(2)
            ],
            axis=0,
        )
        x_high, x_low = split(x)
        y = product(x_high, x_low, fac_high[...], fac_low[...])
        for b in range(2):
            rows_y = y[b * ROWS : (b + 1) * ROWS]
            flat = jnp.concatenate(
                [rows_y[:, g * LANES : (g + 1) * LANES] for g in range(GROUPS)], axis=0
            )
            for p in stream.pieces:
                p.dense[1 + b] = flat[p.start : p.start + p.rows]
        stream.b3_far, stream.b3_recv = arrival(), arrival()
        for p in stream.pieces:
            d, (up, down) = p.dense, p.ways[2]
            remote(d.at[1], d.at[3], up, stream, stream.b3_far)
            remote(d.at[2], d.at[6], down, stream, stream.b3_far)
        for p in stream.pieces:
            d, (up, down) = p.dense, p.ways[2]
            remote(d.at[2], d.at[4], up, stream, stream.b3_recv)
            remote(d.at[1], d.at[5], down, stream, stream.b3_recv)
        here = pl.ds(pl.multiple_of(core * HALF + u * ROWS, ROWS), ROWS)
        out[0, here, :] = jnp.where(core == 0, y[:ROWS], y[ROWS:])
        y_buf[u] = jnp.where(core == 0, y[ROWS:], y[:ROWS])
        last.append(remote(y_buf.at[u], out.at[0, here, :], sibling))

    def b3_far(stream):
        wait_slots(stream, 2, stream.b3_far)
        for p in stream.pieces:
            d, (up, down) = p.dense, p.ways[2]
            remote(d.at[3], d.at[7], up, stream, stream.b3_recv)
            remote(d.at[6], d.at[8], down, stream, stream.b3_recv)

    def b2_start(stream):
        wait_slots(stream, 4, stream.b3_recv)
        stream.b2_far, stream.b2_recv = arrival(), arrival()
        for p in stream.pieces:
            d, (up, down) = p.dense, p.ways[1]
            remote(d.at[pl.ds(1, 4)], d.at[pl.ds(9, 4)], up, stream, stream.b2_far)
            remote(d.at[pl.ds(5, 4)], d.at[pl.ds(21, 4)], down, stream, stream.b2_far)
        for p in stream.pieces:
            d, (up, down) = p.dense, p.ways[1]
            remote(d.at[pl.ds(5, 4)], d.at[pl.ds(13, 4)], up, stream, stream.b2_recv)
            remote(d.at[pl.ds(1, 4)], d.at[pl.ds(17, 4)], down, stream, stream.b2_recv)

    def b2_far(stream):
        wait_slots(stream, 8, stream.b2_far)
        for p in stream.pieces:
            d, (up, down) = p.dense, p.ways[1]
            remote(d.at[pl.ds(9, 4)], d.at[pl.ds(25, 4)], up, stream, stream.b2_recv)
            remote(d.at[pl.ds(21, 4)], d.at[pl.ds(29, 4)], down, stream, stream.b2_recv)

    def answer(p, i):
        return p.dense[tab[p.number, 2, i]]

    def b1_far(stream):
        wait_slots(stream, 16, stream.b2_recv)

        def body(p, h):
            for s in range(3):
                p.b1_far_up[h * 3 + s] = answer(p, 48 + h * 8 + s)
                p.b1_far_down[h * 3 + s] = answer(p, 51 + h * 8 + s)

        loop(stream, 2, body)
        stream.b1_far, stream.b1_recv = arrival(), arrival()
        for p in stream.pieces:
            up, down = p.ways[0]
            remote(p.b1_far_up, p.b1_got_far_up, up, stream, stream.b1_far)
            remote(p.b1_far_down, p.b1_got_far_down, down, stream, stream.b1_far)

    def b1_near(stream):
        def body(p, h):
            for s in range(3):
                p.b1_up[6 + h * 3 + s] = answer(p, 35 + h * 8 + s)
                p.b1_down[h * 3 + s] = answer(p, 16 + h * 8 + s)

        loop(stream, 2, body)
        for p in stream.pieces:
            up, down = p.ways[0]
            remote(p.b1_up.at[pl.ds(6, 6)], p.b1_got.at[pl.ds(6, 6)], up, stream, stream.b1_recv)
            remote(p.b1_down.at[pl.ds(0, 6)], p.b1_got.at[pl.ds(12, 6)], down, stream, stream.b1_recv)

    def b1_merge(stream):
        wait_slots(stream, 12, stream.b1_far)

        def body(p, h):
            for s in range(3):
                p.b1_up[h * 3 + s] = p.b1_got_far_up[h * 3 + s] + answer(p, 32 + h * 8 + s)
                p.b1_down[6 + h * 3 + s] = p.b1_got_far_down[h * 3 + s] + answer(p, 19 + h * 8 + s)

        loop(stream, 2, body)
        for p in stream.pieces:
            up, down = p.ways[0]
            remote(p.b1_up.at[pl.ds(0, 6)], p.b1_got.at[pl.ds(0, 6)], up, stream, stream.b1_recv)
            remote(p.b1_down.at[pl.ds(6, 6)], p.b1_got.at[pl.ds(18, 6)], down, stream, stream.b1_recv)

    def finish(stream):
        u = stream.number
        first = core * HALF + u * ROWS
        wait_slots(stream, 24, stream.b1_recv)

        def body(p, n):
            t, s = n // 3, n % 3
            for h in (1, 0):
                q = t * 6 + h * 3 + s
                value = answer(p, h * 8 + n) + (p.b1_got[q] + p.b1_got[12 + q])
                done = 0
                while done < p.rows:
                    g, r = divmod(p.start + done, ROWS)
                    size = min(ROWS - r, p.rows - done)
                    across = pl.ds(g * LANES, LANES)
                    if h == 0:
                        rows = pl.ds(pl.multiple_of(first + r, 8), size)
                        out[1 + n, rows, across] = value[done : done + size]
                    else:
                        out_buf[u, n, pl.ds(r, size), across] = value[done : done + size]
                    done += size

        loop(stream, SLOTS, body)
        here = pl.ds(pl.multiple_of(first, ROWS), ROWS)
        last.append(remote(out_buf.at[u], out.at[pl.ds(1, SLOTS), here, :], sibling))

    get_col_tab.wait()

    def product_block(k):
        make(k)
        if k == 0:
            waiting["give"].wait_recv()
            send_names(lab.at[0, pl.ds(8, 8)], 8)

    def tables():
        waiting["keep"].wait()
        for j in range(3):
            make_table(j)
        get_factor.wait()
        high, low = split(fac[...])
        fac_high[...] = high
        fac_low[...] = low
        local(tab_v, tab).wait()

    blocks_of = {
        MAKE: product_block, GIVE: send_part, SEND: send_list, PASS_ON: send_far, TABLES: tables,
        NEAR: near_lists, A2_FAR: a2_far, A2_NEAR: a2_near, A2_MERGE: a2_merge, A3: a3_start,
        A3_MERGE: a3_merge, UPDATE: update, B3_FAR: b3_far, B2: b2_start, B2_FAR: b2_far,
        B1_FAR: b1_far, B1_NEAR: b1_near, B1_MERGE: b1_merge, FINISH: finish,
    }
    paced = 0
    for kind, *numbers in ORDER:
        if kind in PACED:
            pl.semaphore_signal(pace_sem, inc=1, device_id=sibling, device_id_type=MESH)
            if paced:
                pl.semaphore_wait(pace_sem, 1)
            paced += 1
        if kind in (MAKE, GIVE, TABLES):
            blocks_of[kind](*numbers)
        else:
            blocks_of[kind](streams[numbers[0]], *numbers[1:])
    pl.semaphore_wait(pace_sem, 1)
    for copy in last:
        copy.wait_recv()
    for copy in sent:
        copy.wait_send()
    for stream in streams:
        assert stream.elements_sent == STREAM_SLOTS * TILE_ROWS * LANES
        ref = blocks.at[:, pl.ds(0, 88), pl.ds(0, 32 * TILE_ROWS)]
        pltpu.make_async_copy(ref, ref, stream.send).wait()


def output_kernel(held, owned, returned, sems):
    copies = (
        pltpu.make_async_copy(held.at[0], owned, sems.at[0]),
        pltpu.make_async_copy(held.at[pl.ds(1, SLOTS)], returned, sems.at[1]),
    )
    for copy in copies:
        copy.start()
    for copy in copies:
        copy.wait()


def local_step(blocks, features, col_ids, row_ids, factor):
    scratch = []
    for u in range(STREAMS):
        for _, rows in PIECES[u]:
            for _, depth in PIECE_BUFFERS:
                scratch.append(pltpu.VMEM((depth, rows, LANES), F32))
    scratch += [
        pltpu.VMEM((RING, B, BPR * B), F32),
        pltpu.VMEM((FT, B, FEAT), F32),
        pltpu.VMEM((FT * B, FEAT), BF16),
        pltpu.VMEM((FT * B, FEAT), BF16),
        pltpu.VMEM((BPR + 1, B, B), F32),
        pltpu.VMEM((B, FT * B), BF16),
        pltpu.VMEM((B, FT * B), BF16),
        pltpu.VMEM((SLOTS, 2, STREAMS, TILE_ROWS, LANES), F32),
        pltpu.VMEM((48, STREAMS, TILE_ROWS, LANES), F32),
        pltpu.VMEM((SLOTS, BPR), I32),
        pltpu.VMEM((16, LANES), I32),
        pltpu.SMEM((16, LANES), I32),
        pltpu.SMEM((SLOTS,), I32),
        pltpu.VMEM((8, LANES), I32),
        pltpu.VMEM((10, 16, LANES), I32),
        pltpu.VMEM((3, 8, LANES), I32),
        pltpu.SMEM((3, 8, LANES), I32),
        pltpu.VMEM((STREAMS, 2, TILE_ROWS, LANES), F32),
        pltpu.VMEM((STREAMS, ROWS, FEAT), F32),
        pltpu.VMEM((STREAMS, SLOTS, ROWS, FEAT), F32),
        pltpu.VMEM((FEAT, FEAT), F32),
        pltpu.VMEM((FEAT, FEAT), BF16),
        pltpu.VMEM((FEAT, FEAT), BF16),
        pltpu.SemaphoreType.DMA((N_SEND,)),
        pltpu.SemaphoreType.DMA((N_RECV,)),
        pltpu.SemaphoreType.DMA((N_LOCAL,)),
        pltpu.SemaphoreType.REGULAR,
    ]
    hbm = pl.BlockSpec(memory_space=pl.ANY)
    held = pl.pallas_call(
        kernel,
        in_specs=[hbm] * 5,
        out_specs=pl.BlockSpec(memory_space=pltpu.VMEM),
        out_shape=pltpu.VMEM((1 + SLOTS, B, FEAT), F32),
        scratch_shapes=scratch,
        compiler_params=pltpu.CompilerParams(
            collective_id=0, has_side_effects=True, vmem_limit_bytes=VMEM_LIMIT
        ),
    )(blocks, features, col_ids, row_ids, factor)
    owned, returned = pl.pallas_call(
        output_kernel,
        in_specs=[pl.BlockSpec(memory_space=pltpu.VMEM)],
        out_specs=[hbm] * 2,
        out_shape=[
            jax.ShapeDtypeStruct((B, FEAT), F32),
            jax.ShapeDtypeStruct((SLOTS, B, FEAT), F32),
        ],
        scratch_shapes=[pltpu.SemaphoreType.DMA((2,))],
        compiler_params=pltpu.CompilerParams(vmem_limit_bytes=1 << 20),
    )(held)
    return owned, returned.reshape(SLOTS * B, FEAT)


def solution(mesh):
    return jax.shard_map(
        local_step,
        mesh=mesh,
        in_specs=(
            P(("gx", "gy"), None, None),
            P(("gx", "gy"), None, None),
            P(("gx", "gy"), None),
            P(("gx", "gy")),
            P(),
        ),
        out_specs=(P(("gx", "gy"), None), P(("gx", "gy"), None)),
        check_vma=False,
    )
```
